512 devices in a mesh: row: 16 (over y_lo, x, core), col: 32 (over y_hi, z).
Axes of the slice: x: 4, y: 4 (y_hi: 2, y_lo: 2; y = y_hi * 2 + y_lo), z: 16, core: 2. Of those that a mesh axis runs over, the one named last changes fastest.
Arguments:
- amplitudes: float32 [8192, 256], P('row', 'col'), may hold values from -6 to 6
- integrals: float32 [256, 8192], P('row', 'col'), may hold values from -0.375 to 0.375
- occ_counts: int32 [8], replicated, may hold values from 1 to 10, 40 in all
- vir_counts: int32 [8], replicated, may hold values from 1 to 80, 400 in all
Outputs:
- symmetrized: float32 [8192, 8192], P('row', 'col')
The draws below stay inside these ranges and needn't reach their ends.
Inputs may be any that keep to these rules, and one draw needn't show every extreme that they name: `occ_counts`: counts of occupied orbitals in the 8 irreducible representations, summing to 40. `vir_counts`: counts of virtual orbitals in the 8 irreducible representations, summing to 400.
All inputs are finite; a program needn't handle non-finite values.
Results may differ from the reference program's by a relative error of at most 0.00007.
Values sent between devices are 32-bit elements; how exact they have to be, the bound alone decides.
A program may use at most 64 MiB of HBM per device.

```python
import math
import jax
import jax.numpy as jnp
import numpy as np
from jax import lax

NOCC = 40
NVIR = 400
IRREPS = 8
KW = 256
PAIRS = 8192


def block_scale(rng, extent, pieces, smallest, top_value):
    factor_of = 1.0
    for position, parts in pieces:
        draws = jax.random.uniform(jax.random.fold_in(jax.random.fold_in(rng, 6), position), (parts,), jnp.float32, smallest / len(pieces), top_value / len(pieces))
        factor_of = factor_of * jnp.repeat(jnp.exp(draws), extent[position] // parts).reshape((-1,) + (1,) * (len(extent) - 1 - position))
    return factor_of


def split_up(number_of, total, reach, lean):
    weights = [(1 << 20) // math.isqrt(grade ** lean) + 1 for grade in range(2, number_of + 1)]
    rest, given = total - reach - (number_of - 1), [1] * (number_of - 1)
    while rest > 0:
        movable = [i for i in range(number_of - 1) if given[i] < reach]
        whole, left = sum([weights[i] for i in movable]), rest
        for i in movable:
            extra = min(reach - given[i], max(1, left * weights[i] // whole), rest)
            given[i] = given[i] + extra
            rest = rest - extra
    return np.array([reach] + given)


def ragged_sizes(own_key, amount, total, bound, lean):
    if amount == 2:
        one = jax.random.randint(own_key, (), max(1, total - bound), min(bound, total - 1) + 1)
        return jnp.stack([one, total - one])
    sizes = jnp.asarray(split_up(amount, total, bound, lean), jnp.int32)
    pairs = (amount - 1) // 2
    source_of, sink = sizes[1:1 + 2 * pairs:2], sizes[2:2 + 2 * pairs:2]
    room = jnp.minimum(source_of - 1, bound - sink)
    shifted = jax.random.randint(jax.random.fold_in(own_key, 1), (pairs,), 0, 1 << 20) % (room + 1)
    sizes = sizes.at[1:1 + 2 * pairs:2].set(source_of - shifted).at[2:2 + 2 * pairs:2].set(sink + shifted)
    return sizes[jax.random.permutation(jax.random.fold_in(own_key, 2), amount)]


def bell_draw(rng, dims, width, most, pieces=(), held_as=jnp.bfloat16):
    gain = block_scale(rng, dims, pieces, -0.22, 0.18) if pieces else 1.0
    array = jax.random.normal(rng, dims, jnp.float32) * width * gain
    return jnp.minimum(jnp.maximum(array, -most), most).astype(held_as)


def setup_inputs(seed: int = 0) -> dict:
    arg_keys = jax.random.split(jax.random.key(seed), 5)
    amplitudes = bell_draw(arg_keys[0], (PAIRS, KW), 1.0, 6.0, ((0, 16), (1, 32)), jnp.float32)
    integrals = bell_draw(arg_keys[1], (KW, PAIRS), KW ** -0.5, 0.375, ((0, 16), (1, 32)), jnp.float32)
    occ_counts = ragged_sizes(arg_keys[2], IRREPS, NOCC, NOCC // 4, 1).astype(jnp.int32)
    vir_counts = ragged_sizes(arg_keys[3], IRREPS, NVIR, NVIR // 5, 1).astype(jnp.int32)
    return {"amplitudes": amplitudes, "integrals": integrals, "occ_counts": occ_counts, "vir_counts": vir_counts}


def orbital_irreps(orbitals, counts):
    bounds = jnp.cumsum(counts)[:-1]
    return jnp.sum((orbitals[:, None] >= bounds[None, :]).astype(jnp.int32), axis=1)


def pair_labels(positions, occ_counts, vir_counts):
    occ_part = orbital_irreps(positions // NVIR, occ_counts)
    vir_part = orbital_irreps(positions % NVIR, vir_counts)
    return jnp.bitwise_xor(occ_part, vir_part)


def reference(amplitudes, integrals, occ_counts, vir_counts):
    cycle = jnp.dot(amplitudes, integrals, precision=lax.Precision.HIGHEST, preferred_element_type=jnp.float32)
    labels = pair_labels(jnp.arange(PAIRS, dtype=jnp.int32), occ_counts, vir_counts)
    allowed = labels[:, None] == labels[None, :]
    return jnp.where(allowed, cycle + cycle.T, 0.0)
```

```python
import jax
import jax.numpy as jnp
from jax import lax
from jax.experimental import pallas as pl
from jax.experimental.pallas import tpu as pltpu
from jax.sharding import PartitionSpec as P

NVIR = 400
MESH = pl.DeviceIdType.MESH
F32 = jnp.float32
BF16 = jnp.bfloat16

TREE = (
    (0x000f1e20, 0x00000fe2, 0x00000001, 0x0000000f, 0x00000003, 0x0000012e, 0x00000fe4, 0x0000000d,
     0x00000005, 0x0000012c, 0x000000f6, 0x0000000b, 0x0000012a, 0x00000007, 0x00000009, 0x00000008),
    (0x11102f31, 0x11111112, 0x111110f3, 0x11111110, 0x1111123f, 0x11111114, 0x111110f5, 0x1111111e,
     0x1111123d, 0x11111116, 0x11111107, 0x1111111c, 0x1111123b, 0x11111118, 0x1111111a, 0x11111119),
    (0x22213042, 0x22222223, 0x22222104, 0x22222221, 0x22222340, 0x22222225, 0x22222106, 0x2222222f,
     0x2222234e, 0x22222227, 0x22222218, 0x2222222d, 0x2222234c, 0x22222229, 0x2222222b, 0x2222222a),
    (0x33324153, 0x33333332, 0x33333334, 0x33333215, 0x33333451, 0x33333336, 0x33333330, 0x33333217,
     0x3333345f, 0x3333333e, 0x33333338, 0x3333345d, 0x33333329, 0x3333333a, 0x3333333c, 0x3333333b),
    (0x44435264, 0x44444562, 0x44444443, 0x44444445, 0x44444326, 0x44444441, 0x44444560, 0x44444447,
     0x44444328, 0x4444444f, 0x4444456e, 0x44444449, 0x4444443a, 0x4444444d, 0x4444444c, 0x4444444b),
    (0x55546375, 0x55555554, 0x55555673, 0x55555552, 0x55555556, 0x55555437, 0x55555671, 0x55555558,
     0x55555439, 0x55555550, 0x5555567f, 0x5555555a, 0x5555554b, 0x5555555c, 0x5555555e, 0x5555555d),
    (0x66657486, 0x66666784, 0x66666665, 0x66666782, 0x66666667, 0x66666548, 0x66666663, 0x66666669,
     0x6666654a, 0x66666661, 0x66666780, 0x6666665c, 0x6666666b, 0x6666666d, 0x6666666f, 0x6666666e),
    (0x77768597, 0x77777895, 0x77777776, 0x77777778, 0x77777774, 0x77777659, 0x77777893, 0x77777772,
     0x7777777a, 0x77777891, 0x7777765b, 0x7777777c, 0x7777776d, 0x77777770, 0x7777777f, 0x7777777e),
    (0x888796a8, 0x88888887, 0x888889a6, 0x88888889, 0x888889a4, 0x8888876a, 0x88888885, 0x888889a2,
     0x8888876c, 0x8888888b, 0x88888883, 0x8888888d, 0x8888887e, 0x88888881, 0x88888880, 0x8888888f),
    (0x9998a7b9, 0x99999ab7, 0x9999999a, 0x99999998, 0x9999987b, 0x99999ab5, 0x9999999c, 0x99999996,
     0x9999987d, 0x99999994, 0x99999ab3, 0x99999992, 0x9999999e, 0x99999991, 0x9999998f, 0x99999990),
    (0xaaa9b8ca, 0xaaaaa98c, 0xaaaaaaa9, 0xaaaaabc8, 0xaaaaaaab, 0xaaaaaaa7, 0xaaaaabc6, 0xaaaaaaad,
     0xaaaaa98e, 0xaaaaabc4, 0xaaaaaaa5, 0xaaaaaaa2, 0xaaaaaaaf, 0xaaaaaa90, 0xaaaaaaa3, 0xaaaaaaa1),
    (0xbbbac9db, 0xbbbbbbbc, 0xbbbbbbba, 0xbbbbba9d, 0xbbbbbcd9, 0xbbbbbcd7, 0xbbbbbbbe, 0xbbbbbbb8,
     0xbbbbba9f, 0xbbbbbbb2, 0xbbbbbcd5, 0xbbbbbbb6, 0xbbbbbbb0, 0xbbbbbba1, 0xbbbbbbb4, 0xbbbbbbb3),
    (0xcccbdaec, 0xcccccccd, 0xcccccccb, 0xcccccbae, 0xcccccdea, 0xccccccb2, 0xcccccccf, 0xccccccc9,
     0xcccccba0, 0xcccccde8, 0xccccccc7, 0xcccccde6, 0xccccccc1, 0xccccccc4, 0xccccccc3, 0xccccccc5),
    (0xdddcebfd, 0xdddddddc, 0xddddddde, 0xdddddefb, 0xdddddcbf, 0xddddddd2, 0xddddddd0, 0xddddddda,
     0xdddddcb1, 0xdddddef9, 0xddddddc3, 0xdddddef7, 0xddddddd4, 0xddddddd8, 0xddddddd5, 0xddddddd6),
    (0xeeedfc0e, 0xeeeeedc2, 0xeeeeeeed, 0xeeeeeeef, 0xeeeeef0c, 0xeeeeedc0, 0xeeeeeeeb, 0xeeeeeee1,
     0xeeeeef0a, 0xeeeeeed4, 0xeeeeeee3, 0xeeeeeee5, 0xeeeeeee9, 0xeeeeef08, 0xeeeeeee7, 0xeeeeeee6),
    (0xfffe0d1f, 0xfffffff2, 0xfffffffe, 0xfffffff0, 0xfffff01d, 0xfffffed1, 0xfffffed3, 0xfffffffc,
     0xfffffff4, 0xfffff01b, 0xffffffe5, 0xfffffffa, 0xfffffff6, 0xfffff019, 0xfffffff7, 0xfffffff8),
)

def signed(word):
    return word - (1 << 32) if word >= 1 << 31 else word


def by_z(z, values):
    picked = jnp.int32(signed(values[0]))
    for k in range(1, 16):
        if values[k] != values[0]:
            picked = jnp.where(z == k, jnp.int32(signed(values[k])), picked)
    return picked


def nibble(word, k):
    return (word >> (4 * k)) & 15


def targets(z):
    found = []
    for word in TREE[z]:
        for k in range(1, 8):
            d = (word >> (4 * k)) & 15
            if d != z and d not in found:
                found.append(d)
    return found


SENDS = [sum((word >> (4 * k)) & 15 != z for word in TREE[z] for k in range(1, 8)) for z in range(16)]
MOST = max(SENDS)
TARGETS = [len(targets(z)) for z in range(16)]
SOURCES = [sum(1 << z for z in range(16) if d in targets(z)) for d in range(16)]


def labels(position, base, occ, vir):
    first = base // NVIR
    orbital = jnp.full_like(position, first)
    for k in (1, 2):
        orbital += (position >= (first + k) * NVIR).astype(jnp.int32)
    virtual = position - orbital * NVIR
    occ_part = jnp.zeros_like(position)
    vir_part = jnp.zeros_like(position)
    occ_bound = jnp.int32(0)
    vir_bound = jnp.int32(0)
    for k in range(7):
        occ_bound += occ[k]
        vir_bound += vir[k]
        occ_part += (orbital >= occ_bound).astype(jnp.int32)
        vir_part += (virtual >= vir_bound).astype(jnp.int32)
    return occ_part ^ vir_part


def split(x):
    high = x.astype(BF16)
    return high, (x - high.astype(F32)).astype(BF16)


def product(left, right):
    dims = (((0,), (0,)), ((), ()))
    lh, ll = split(left)
    rh, rl = split(right)
    dot = lambda a, b: lax.dot_general(a, b, dims, preferred_element_type=F32)
    return dot(lh, rh) + (dot(lh, rl) + dot(ll, rh))


def kernel(
    a_hbm, b_hbm, occ, vir, o_ref,
    at, bz, br, bc, ac, row_lab,
    local, at_in, bz_in, br_in, bc_in, ac_in, tree_out, cross_out, br_out, bc_out, ac_out,
):
    row = lax.axis_index("row")
    col = lax.axis_index("col")
    z = col % 16
    yhi = col // 16
    ylo = row // 8

    own = [
        pltpu.make_async_copy(a_hbm.at[:, pl.ds(0, 256)], at.at[col, 0], local.at[0]),
        pltpu.make_async_copy(a_hbm.at[:, pl.ds(256, 256)], at.at[col, 1], local.at[1]),
        pltpu.make_async_copy(b_hbm, bz.at[z], local.at[2]),
        pltpu.make_async_copy(b_hbm, bc.at[row], local.at[3]),
    ]
    for copy in own:
        copy.start()

    barrier = pltpu.get_barrier_semaphore()
    sources = by_z(z, SOURCES)

    def greet_z(d, carry):
        @pl.when(((sources >> d) & 1) == 1)
        def _():
            pl.semaphore_signal(
                barrier, inc=1, device_id={"row": row, "col": yhi * 16 + d}, device_id_type=MESH
            )
        return carry

    def greet_plane(t, carry):
        r, y = t % 16, t // 16

        @pl.when(jnp.logical_or(r != row, y != yhi))
        def _():
            pl.semaphore_signal(
                barrier, inc=1, device_id={"row": r, "col": y * 16 + z}, device_id_type=MESH
            )
        return carry

    lax.fori_loop(0, 16, greet_z, 0)
    lax.fori_loop(0, 32, greet_plane, 0)

    row_pos = row * 512 + lax.broadcasted_iota(jnp.int32, (512, 128), 0)
    row_lab[...] = labels(row_pos, row * 512, occ, vir)

    pl.semaphore_wait(barrier, 31 + by_z(z, TARGETS))
    for copy in own:
        copy.wait()

    def send_tree(s, d, j):
        c = yhi * 16 + s
        dev = {"row": row, "col": yhi * 16 + d}
        pltpu.make_async_remote_copy(
            src_ref=at.at[c], dst_ref=at.at[c], send_sem=tree_out.at[j], recv_sem=at_in.at[c],
            device_id=dev, device_id_type=MESH,
        ).start()
        pltpu.make_async_remote_copy(
            src_ref=bz.at[s], dst_ref=bz.at[s], send_sem=tree_out.at[MOST + j], recv_sem=bz_in.at[s],
            device_id=dev, device_id_type=MESH,
        ).start()

    def cross(s):
        c = yhi * 16 + s
        return pltpu.make_async_remote_copy(
            src_ref=at.at[c], dst_ref=at.at[c], send_sem=cross_out.at[s], recv_sem=at_in.at[c],
            device_id={"row": row, "col": (1 - yhi) * 16 + z}, device_id_type=MESH,
        )

    def to_rows(s, y):
        return pltpu.make_async_remote_copy(
            src_ref=bz.at[s], dst_ref=br.at[row, s % 2], send_sem=br_out.at[2 * s + y],
            recv_sem=br_in.at[2 * row + s % 2],
            device_id={"row": yhi * 8 + s // 2, "col": y * 16 + z}, device_id_type=MESH,
        )

    def mine(s, y):
        return jnp.logical_and(yhi * 8 + s // 2 == row, y == yhi)

    owner = row % 8 == z // 2
    half = z % 2

    def to_plane(s, r):
        c = yhi * 16 + s
        return pltpu.make_async_remote_copy(
            src_ref=at.at[c, half], dst_ref=ac.at[c], send_sem=ac_out.at[16 * s + r], recv_sem=ac_in.at[c],
            device_id={"row": r, "col": ylo * 16 + z}, device_id_type=MESH,
        )

    def own_plane(r):
        return jnp.logical_and(r == row, ylo == yhi)

    def spread(s):
        cross(s).start()
        for y in (0, 1):
            me = mine(s, y)

            @pl.when(me)
            def _():
                pltpu.make_async_copy(bz.at[s], br.at[row, s % 2], br_in.at[2 * row + s % 2]).start()

            @pl.when(jnp.logical_not(me))
            def _():
                to_rows(s, y).start()

        @pl.when(owner)
        def _():
            def one(r, carry):
                me = own_plane(r)

                @pl.when(me)
                def _():
                    c = yhi * 16 + s
                    pltpu.make_async_copy(at.at[c, half], ac.at[c], ac_in.at[c]).start()

                @pl.when(jnp.logical_not(me))
                def _():
                    to_plane(s, r).start()
                return carry

            lax.fori_loop(0, 16, one, 0)

    def to_col(r):
        return pltpu.make_async_remote_copy(
            src_ref=bz.at[z], dst_ref=bc.at[row], send_sem=bc_out.at[r], recv_sem=bc_in.at[row],
            device_id={"row": r, "col": col}, device_id_type=MESH,
        )

    sent = jnp.int32(0)
    for k in range(16):
        word = by_z(z, [TREE[v][k] for v in range(16)])
        s = nibble(word, 0)
        c = yhi * 16 + s
        if k:
            pltpu.make_async_copy(at.at[c], at.at[c], at_in.at[c]).wait()
            pltpu.make_async_copy(bz.at[s], bz.at[s], bz_in.at[s]).wait()

        def forward(i, j):
            d = (word >> (4 * i)) & 15
            there = d != z

            @pl.when(there)
            def _():
                send_tree(s, d, j)
            return j + there.astype(jnp.int32)

        sent = lax.fori_loop(1, 8, forward, sent)
        spread(s)
        if k == 0:
            def give(r, carry):
                @pl.when(r != row)
                def _():
                    to_col(r).start()
                return carry

            lax.fori_loop(0, 16, give, 0)

    def rest(t, carry):
        @pl.when(t != row)
        def _():
            pltpu.make_async_copy(bc.at[t], bc.at[t], bc_in.at[t]).wait()
        c = (1 - yhi) * 16 + t
        pltpu.make_async_copy(at.at[c], at.at[c], at_in.at[c]).wait()
        for e in (0, 1):
            pltpu.make_async_copy(br.at[t, e], br.at[t, e], br_in.at[2 * t + e]).wait()
            pltpu.make_async_copy(ac.at[2 * t + e], ac.at[2 * t + e], ac_in.at[2 * t + e]).wait()
        return carry

    lax.fori_loop(0, 16, rest, 0)

    col_lab = labels(
        col * 256 + lax.broadcasted_iota(jnp.int32, (8, 256), 1), col * 256, occ, vir
    )[:1]
    b_here = bc[...].reshape(256, 256)
    a_here = ac[...].reshape(256, 256)
    for m in (0, 1):
        rows = slice(256 * m, 256 * (m + 1))
        total = product(at[:, m].reshape(256, 256), b_here) + product(br[:, m].reshape(256, 256), a_here)
        lab = row_lab[rows]
        for h in (0, 1):
            lanes = slice(128 * h, 128 * (h + 1))
            o_ref[rows, lanes] = jnp.where(lab == col_lab[:, lanes], total[:, lanes], 0.0)

    def sent_tree(j, carry):
        pltpu.make_async_copy(at.at[0], at.at[0], tree_out.at[j]).wait()
        pltpu.make_async_copy(bz.at[0], bz.at[0], tree_out.at[MOST + j]).wait()
        return carry

    lax.fori_loop(0, by_z(z, SENDS), sent_tree, 0)

    def sent_plane(s, carry):
        cross(s).wait_send()
        for y in (0, 1):
            @pl.when(jnp.logical_not(mine(s, y)))
            def _():
                to_rows(s, y).wait_send()

        @pl.when(s != row)
        def _():
            to_col(s).wait_send()

        @pl.when(owner)
        def _():
            def one(r, carry):
                @pl.when(jnp.logical_not(own_plane(r)))
                def _():
                    to_plane(s, r).wait_send()
                return carry

            lax.fori_loop(0, 16, one, 0)
        return carry

    lax.fori_loop(0, 16, sent_plane, 0)


def per_device(amplitudes, integrals, occ_counts, vir_counts):
    any_space = pl.BlockSpec(memory_space=pl.ANY)
    scalars = pl.BlockSpec(memory_space=pltpu.SMEM)
    dma = pltpu.SemaphoreType.DMA
    return pl.pallas_call(
        kernel,
        out_shape=jax.ShapeDtypeStruct((512, 256), F32),
        in_specs=[any_space, any_space, scalars, scalars],
        out_specs=pl.BlockSpec(memory_space=pltpu.VMEM),
        scratch_shapes=[
            pltpu.VMEM((32, 2, 8, 256), F32),
            pltpu.VMEM((16, 16, 256), F32),
            pltpu.VMEM((16, 2, 16, 256), F32),
            pltpu.VMEM((16, 16, 256), F32),
            pltpu.VMEM((32, 8, 256), F32),
            pltpu.VMEM((512, 128), jnp.int32),
            dma((4,)), dma((32,)), dma((16,)), dma((32,)), dma((16,)), dma((32,)),
            dma((2 * MOST,)), dma((16,)), dma((32,)), dma((16,)), dma((256,)),
        ],
        compiler_params=pltpu.CompilerParams(
            collective_id=0, has_side_effects=True, vmem_limit_bytes=32 * 2**20
        ),
    )(amplitudes.T, integrals, occ_counts, vir_counts)


def solution(mesh):
    placed = (P("row", "col"), P("row", "col"), P(), P())
    return jax.shard_map(
        per_device, mesh=mesh, in_specs=placed, out_specs=P("row", "col"), check_vma=False
    )
```

```python
import jax
import jax.numpy as jnp
from jax import lax
from jax.experimental import pallas as pl
from jax.experimental.pallas import tpu as pltpu
from jax.sharding import PartitionSpec as P

NVIR = 400
MESH = pl.DeviceIdType.MESH
F32 = jnp.float32
BF16 = jnp.bfloat16

TREE = (
    (0x000f1e20, 0x00000fe2, 0x00000001, 0x0000000f, 0x00000003, 0x0000012e, 0x00000fe4, 0x0000000d,
     0x00000005, 0x0000012c, 0x000000f6, 0x0000000b, 0x0000012a, 0x00000007, 0x00000009, 0x00000008),
    (0x11102f31, 0x11111112, 0x111110f3, 0x11111110, 0x1111123f, 0x11111114, 0x111110f5, 0x1111111e,
     0x1111123d, 0x11111116, 0x11111107, 0x1111111c, 0x1111123b, 0x11111118, 0x1111111a, 0x11111119),
    (0x22213042, 0x22222223, 0x22222104, 0x22222221, 0x22222340, 0x22222225, 0x22222106, 0x2222222f,
     0x2222234e, 0x22222227, 0x22222218, 0x2222222d, 0x2222234c, 0x22222229, 0x2222222b, 0x2222222a),
    (0x33324153, 0x33333332, 0x33333334, 0x33333215, 0x33333451, 0x33333336, 0x33333330, 0x33333217,
     0x3333345f, 0x3333333e, 0x33333338, 0x3333345d, 0x33333329, 0x3333333a, 0x3333333c, 0x3333333b),
    (0x44435264, 0x44444562, 0x44444443, 0x44444445, 0x44444326, 0x44444441, 0x44444560, 0x44444447,
     0x44444328, 0x4444444f, 0x4444456e, 0x44444449, 0x4444443a, 0x4444444d, 0x4444444c, 0x4444444b),
    (0x55546375, 0x55555554, 0x55555673, 0x55555552, 0x55555556, 0x55555437, 0x55555671, 0x55555558,
     0x55555439, 0x55555550, 0x5555567f, 0x5555555a, 0x5555554b, 0x5555555c, 0x5555555e, 0x5555555d),
    (0x66657486, 0x66666784, 0x66666665, 0x66666782, 0x66666667, 0x66666548, 0x66666663, 0x66666669,
     0x6666654a, 0x66666661, 0x66666780, 0x6666665c, 0x6666666b, 0x6666666d, 0x6666666f, 0x6666666e),
    (0x77768597, 0x77777895, 0x77777776, 0x77777778, 0x77777774, 0x77777659, 0x77777893, 0x77777772,
     0x7777777a, 0x77777891, 0x7777765b, 0x7777777c, 0x7777776d, 0x77777770, 0x7777777f, 0x7777777e),
    (0x888796a8, 0x88888887, 0x888889a6, 0x88888889, 0x888889a4, 0x8888876a, 0x88888885, 0x888889a2,
     0x8888876c, 0x8888888b, 0x88888883, 0x8888888d, 0x8888887e, 0x88888881, 0x88888880, 0x8888888f),
    (0x9998a7b9, 0x99999ab7, 0x9999999a, 0x99999998, 0x9999987b, 0x99999ab5, 0x9999999c, 0x99999996,
     0x9999987d, 0x99999994, 0x99999ab3, 0x99999992, 0x9999999e, 0x99999991, 0x9999998f, 0x99999990),
    (0xaaa9b8ca, 0xaaaaa98c, 0xaaaaaaa9, 0xaaaaabc8, 0xaaaaaaab, 0xaaaaaaa7, 0xaaaaabc6, 0xaaaaaaad,
     0xaaaaa98e, 0xaaaaabc4, 0xaaaaaaa5, 0xaaaaaaa2, 0xaaaaaaaf, 0xaaaaaa90, 0xaaaaaaa3, 0xaaaaaaa1),
    (0xbbbac9db, 0xbbbbbbbc, 0xbbbbbbba, 0xbbbbba9d, 0xbbbbbcd9, 0xbbbbbcd7, 0xbbbbbbbe, 0xbbbbbbb8,
     0xbbbbba9f, 0xbbbbbbb2, 0xbbbbbcd5, 0xbbbbbbb6, 0xbbbbbbb0, 0xbbbbbba1, 0xbbbbbbb4, 0xbbbbbbb3),
    (0xcccbdaec, 0xcccccccd, 0xcccccccb, 0xcccccbae, 0xcccccdea, 0xccccccb2, 0xcccccccf, 0xccccccc9,
     0xcccccba0, 0xcccccde8, 0xccccccc7, 0xcccccde6, 0xccccccc1, 0xccccccc4, 0xccccccc3, 0xccccccc5),
    (0xdddcebfd, 0xdddddddc, 0xddddddde, 0xdddddefb, 0xdddddcbf, 0xddddddd2, 0xddddddd0, 0xddddddda,
     0xdddddcb1, 0xdddddef9, 0xddddddc3, 0xdddddef7, 0xddddddd4, 0xddddddd8, 0xddddddd5, 0xddddddd6),
    (0xeeedfc0e, 0xeeeeedc2, 0xeeeeeeed, 0xeeeeeeef, 0xeeeeef0c, 0xeeeeedc0, 0xeeeeeeeb, 0xeeeeeee1,
     0xeeeeef0a, 0xeeeeeed4, 0xeeeeeee3, 0xeeeeeee5, 0xeeeeeee9, 0xeeeeef08, 0xeeeeeee7, 0xeeeeeee6),
    (0xfffe0d1f, 0xfffffff2, 0xfffffffe, 0xfffffff0, 0xfffff01d, 0xfffffed1, 0xfffffed3, 0xfffffffc,
     0xfffffff4, 0xfffff01b, 0xffffffe5, 0xfffffffa, 0xfffffff6, 0xfffff019, 0xfffffff7, 0xfffffff8),
)

def signed(word):
    return word - (1 << 32) if word >= 1 << 31 else word


def by_z(z, values):
    picked = jnp.int32(signed(values[0]))
    for k in range(1, 16):
        if values[k] != values[0]:
            picked = jnp.where(z == k, jnp.int32(signed(values[k])), picked)
    return picked


def nibble(word, k):
    return (word >> (4 * k)) & 15


def quarter(word):
    first = word & 12
    return range(first, first + 4)


def targets(z):
    found = []
    for word in TREE[z]:
        for k in range(1, 8):
            d = (word >> (4 * k)) & 15
            if d != z and d not in found:
                found.append(d)
    return found


SENDS = [sum((word >> (4 * k)) & 15 != z for word in TREE[z] for k in range(1, 8)) for z in range(16)]
MOST = max(SENDS)
TARGETS = [len(targets(z)) for z in range(16)]
LAST = [
    sum(1 << k for k in range(16) if all(TREE[z][i] & 15 != q for i in range(k + 1, 16) for q in quarter(TREE[z][k])))
    for z in range(16)
]
GROUPS = (0, 1, 3, 2)
SOURCES = [sum(1 << z for z in range(16) if d in targets(z)) for d in range(16)]


def labels(position, base, occ, vir):
    first = base // NVIR
    orbital = jnp.full_like(position, first)
    for k in (1, 2):
        orbital += (position >= (first + k) * NVIR).astype(jnp.int32)
    virtual = position - orbital * NVIR
    occ_part = jnp.zeros_like(position)
    vir_part = jnp.zeros_like(position)
    occ_bound = jnp.int32(0)
    vir_bound = jnp.int32(0)
    for k in range(7):
        occ_bound += occ[k]
        vir_bound += vir[k]
        occ_part += (orbital >= occ_bound).astype(jnp.int32)
        vir_part += (virtual >= vir_bound).astype(jnp.int32)
    return occ_part ^ vir_part


def split(x):
    high = x.astype(BF16)
    return high, (x - high.astype(F32)).astype(BF16)


def product(left, right):
    dims = (((0,), (0,)), ((), ()))
    lh, ll = split(left)
    rh, rl = split(right)
    dot = lambda a, b: lax.dot_general(a, b, dims, preferred_element_type=F32)
    return dot(lh, rh) + (dot(lh, rl) + dot(ll, rh))


def kernel(
    a_hbm, b_hbm, occ_hbm, vir_hbm, o_ref,
    w, br, bc, ac, row_lab, occ, vir,
    local, w_in, br_in, bc_in, ac_in, cross_in,
    tree_out, cross_out, br_out, bc_out, ac_out, pair_out,
):
    row = lax.axis_index("row")
    col = lax.axis_index("col")
    z = col % 16
    yhi = col // 16
    ylo = row // 8
    core = row % 2

    own = [
        pltpu.make_async_copy(a_hbm.at[:, pl.ds(256 * h, 256)], w.at[col, h], local.at[h])
        for h in (0, 1)
    ] + [
        pltpu.make_async_copy(b_hbm.at[pl.ds(8 * h, 8)], w.at[col, 2 + h], local.at[2 + h])
        for h in (0, 1)
    ]
    small = [
        pltpu.make_async_copy(occ_hbm, occ, local.at[4]),
        pltpu.make_async_copy(vir_hbm, vir, local.at[5]),
        pltpu.make_async_copy(b_hbm.at[pl.ds(0, 8)], bc.at[row, 0], local.at[6]),
        pltpu.make_async_copy(b_hbm.at[pl.ds(8, 8)], bc.at[row, 1], local.at[7]),
    ]
    for copy in own + small:
        copy.start()

    barrier = pltpu.get_barrier_semaphore()
    sources = by_z(z, SOURCES)

    def greet_z(d, carry):
        @pl.when(((sources >> d) & 1) == 1)
        def _():
            pl.semaphore_signal(
                barrier, inc=1, device_id={"row": row, "col": yhi * 16 + d}, device_id_type=MESH
            )
        return carry

    def greet_plane(t, carry):
        r, y = t % 16, t // 16

        @pl.when(jnp.logical_or(r != row, y != yhi))
        def _():
            pl.semaphore_signal(
                barrier, inc=1, device_id={"row": r, "col": y * 16 + z}, device_id_type=MESH
            )
        return carry

    lax.fori_loop(0, 32, greet_plane, 0)
    lax.fori_loop(0, 16, greet_z, 0)

    pl.semaphore_wait(barrier, 31 + by_z(z, TARGETS))
    for copy in own:
        copy.wait()

    def send_tree(s, d, j):
        c = yhi * 16 + s
        pltpu.make_async_remote_copy(
            src_ref=w.at[c], dst_ref=w.at[c], send_sem=tree_out.at[j], recv_sem=w_in.at[s],
            device_id={"row": row, "col": yhi * 16 + d}, device_id_type=MESH,
        ).start()

    def cross(s):
        c = yhi * 16 + s
        return pltpu.make_async_remote_copy(
            src_ref=w.at[c, pl.ds(0, 2)], dst_ref=w.at[c, pl.ds(0, 2)], send_sem=cross_out,
            recv_sem=cross_in, device_id={"row": row, "col": (1 - yhi) * 16 + z}, device_id_type=MESH,
        )

    def to_rows(s, y):
        r = yhi * 8 + s // 2
        source = w.at[yhi * 16 + s, pl.ds(2, 2)]
        me = jnp.logical_and(r == row, y == yhi)

        @pl.when(me)
        def _():
            pltpu.make_async_copy(source, br.at[row, s % 2], br_in).start()

        @pl.when(jnp.logical_not(me))
        def _():
            pltpu.make_async_remote_copy(
                src_ref=source, dst_ref=br.at[row, s % 2], send_sem=br_out, recv_sem=br_in,
                device_id={"row": r, "col": y * 16 + z}, device_id_type=MESH,
            ).start()

    owner = row % 8 == z // 2
    half = z % 2

    def to_plane(g):
        c = yhi * 16 + 4 * g
        source = w.at[pl.ds(c, 4), half]

        def one(chip, carry):
            r = 2 * chip + core
            me = jnp.logical_and(r == row, ylo == yhi)

            @pl.when(me)
            def _():
                pltpu.make_async_copy(source, ac.at[pl.ds(c, 4)], ac_in.at[yhi * 4 + g]).start()

            @pl.when(jnp.logical_not(me))
            def _():
                pltpu.make_async_remote_copy(
                    src_ref=source, dst_ref=ac.at[pl.ds(c, 4)], send_sem=ac_out.at[g],
                    recv_sem=ac_in.at[yhi * 4 + g],
                    device_id={"row": r, "col": ylo * 16 + z}, device_id_type=MESH,
                ).start()
            return carry

        lax.fori_loop(0, 8, one, 0)

    last = by_z(z, LAST)
    sent = jnp.int32(0)
    for k in range(16):
        word = by_z(z, [TREE[v][k] for v in range(16)])
        s = nibble(word, 0)
        if k:
            pltpu.make_async_copy(w.at[s], w.at[s], w_in.at[s]).wait()

        def forward(i, j):
            d = (word >> (4 * i)) & 15
            there = d != z

            @pl.when(there)
            def _():
                send_tree(s, d, j)
            return j + there.astype(jnp.int32)

        sent = lax.fori_loop(1, 8, forward, sent)
        cross(s).start()
        to_rows(s, 0)
        to_rows(s, 1)

        @pl.when(jnp.logical_and(owner, ((last >> k) & 1) == 1))
        def _():
            to_plane(s // 4)

        if k == 0:
            def give(r, carry):
                @pl.when(r != row)
                def _():
                    pltpu.make_async_remote_copy(
                        src_ref=w.at[col, pl.ds(2, 2)], dst_ref=bc.at[row], send_sem=bc_out,
                        recv_sem=bc_in, device_id={"row": r, "col": col}, device_id_type=MESH,
                    ).start()
                return carry

            lax.fori_loop(0, 16, give, 0)
            for copy in small:
                copy.wait()
            row_pos = row * 512 + lax.broadcasted_iota(jnp.int32, (512, 128), 0)
            row_lab[...] = labels(row_pos, row * 512, occ, vir)

    first = core == (z // 2) % 2

    def group(t):
        return ac.at[pl.ds(4 * t, 4)]

    @pl.when(first)
    def _():
        for g in GROUPS:
            for y in (0, 1):
                t = 4 * y + g
                pltpu.make_async_copy(group(t), group(t), ac_in.at[t]).wait()
                pltpu.make_async_remote_copy(
                    src_ref=group(t), dst_ref=group(t), send_sem=pair_out.at[t],
                    recv_sem=ac_in.at[t], device_id={"row": 2 * (row // 2) + 1 - core, "col": col},
                    device_id_type=MESH,
                ).start()

    pltpu.make_async_copy(bc.at[pl.ds(0, 15)], bc.at[pl.ds(0, 15)], bc_in).wait()
    pltpu.make_async_copy(ac, ac, cross_in).wait()
    pltpu.make_async_copy(br, br, br_in).wait()

    @pl.when(jnp.logical_not(first))
    def _():
        for t in range(8):
            pltpu.make_async_copy(group(t), group(t), ac_in.at[t]).wait()

    col_lab = labels(
        col * 256 + lax.broadcasted_iota(jnp.int32, (8, 256), 1), col * 256, occ, vir
    )[:1]
    b_here = bc[...].reshape(256, 256)
    a_here = ac[...].reshape(256, 256)
    for m in (0, 1):
        rows = slice(256 * m, 256 * (m + 1))
        total = product(w[:, m].reshape(256, 256), b_here) + product(br[:, m].reshape(256, 256), a_here)
        lab = row_lab[rows]
        for h in (0, 1):
            lanes = slice(128 * h, 128 * (h + 1))
            o_ref[rows, lanes] = jnp.where(lab == col_lab[:, lanes], total[:, lanes], 0.0)

    def sent_tree(j, carry):
        pltpu.make_async_copy(w.at[0], w.at[0], tree_out.at[j]).wait()
        return carry

    lax.fori_loop(0, by_z(z, SENDS), sent_tree, 0)
    pltpu.make_async_copy(ac, ac, cross_out).wait()
    pltpu.make_async_copy(bc.at[pl.ds(0, 15)], bc.at[pl.ds(0, 15)], bc_out).wait()

    @pl.when(ylo == yhi)
    def _():
        pltpu.make_async_copy(br.at[pl.ds(0, 15)], br.at[pl.ds(0, 15)], br_out).wait()

    @pl.when(ylo != yhi)
    def _():
        pltpu.make_async_copy(br, br, br_out).wait()

    @pl.when(owner)
    def _():
        for g in range(4):
            @pl.when(ylo == yhi)
            def _():
                pltpu.make_async_copy(ac.at[pl.ds(0, 28)], ac.at[pl.ds(0, 28)], ac_out.at[g]).wait()

            @pl.when(ylo != yhi)
            def _():
                pltpu.make_async_copy(ac, ac, ac_out.at[g]).wait()

    @pl.when(first)
    def _():
        for t in range(8):
            pltpu.make_async_copy(group(t), group(t), pair_out.at[t]).wait()


def per_device(amplitudes, integrals, occ_counts, vir_counts):
    arrays = (amplitudes.T, integrals, occ_counts, vir_counts)
    hbm = pl.BlockSpec(memory_space=pltpu.HBM)
    dma = pltpu.SemaphoreType.DMA
    return pl.pallas_call(
        kernel,
        out_shape=jax.ShapeDtypeStruct((512, 256), F32),
        in_specs=[hbm, hbm, hbm, hbm],
        out_specs=pl.BlockSpec(memory_space=pltpu.VMEM),
        scratch_shapes=[
            pltpu.VMEM((32, 4, 8, 256), F32),
            pltpu.VMEM((16, 2, 2, 8, 256), F32),
            pltpu.VMEM((16, 2, 8, 256), F32),
            pltpu.VMEM((32, 8, 256), F32),
            pltpu.VMEM((512, 128), jnp.int32),
            pltpu.SMEM((8,), jnp.int32),
            pltpu.SMEM((8,), jnp.int32),
            dma((8,)), dma((16,)), dma, dma, dma((8,)), dma,
            dma((MOST,)), dma, dma, dma, dma((4,)), dma((8,)),
        ],
        compiler_params=pltpu.CompilerParams(
            collective_id=0, has_side_effects=True, vmem_limit_bytes=32 * 2**20
        ),
    )(*[pltpu.with_memory_space_constraint(v, pltpu.HBM) for v in arrays])


def solution(mesh):
    placed = (P("row", "col"), P("row", "col"), P(), P())
    return jax.shard_map(
        per_device, mesh=mesh, in_specs=placed, out_specs=P("row", "col"), check_vma=False
    )
```

```python
import jax
import jax.numpy as jnp
from jax import lax
from jax.experimental import pallas as pl
from jax.experimental.pallas import tpu as pltpu
from jax.sharding import PartitionSpec as P

NVIR = 400
SPAN = 2
MESH = pl.DeviceIdType.MESH
F32 = jnp.float32
BF16 = jnp.bfloat16

TREE = (
    (0x0000dc20, 0x000002cf, 0x000000f4, 0x000000d2, 0x0000031d, 0x0000e21b, 0x000000f3, 0x000000f6,
     0x0000001a, 0x0000000e, 0x00000018, 0x000000d5, 0x00000001, 0x0000000c, 0x00000009, 0x00000007),
    (0x11124bf1, 0x11111112, 0x1111204e, 0x11111105, 0x111d320c, 0x11111114, 0x11111119, 0x11111110,
     0x1111112d, 0x11111113, 0x111113db, 0x1111116f, 0x111111d6, 0x1111111a, 0x11111118, 0x111111f7),
    (0x22213042, 0x22222214, 0x22223510, 0x22222213, 0x22222221, 0x22222136, 0x2222222f, 0x22222235,
     0x22222228, 0x2222222e, 0x222222f9, 0x222222ec, 0x2222222b, 0x22222227, 0x2222222d, 0x2222222a),
    (0x33504623, 0x33333334, 0x33333382, 0x3333351f, 0x33321407, 0x33333348, 0x33333330, 0x33333339,
     0x33333346, 0x33333331, 0x3333334d, 0x333333fa, 0x33333335, 0x3333333c, 0x3333333e, 0x3333333b),
    (0x44532604, 0x44444425, 0x44444462, 0x44444443, 0x44447531, 0x4444235a, 0x4444653e, 0x44444449,
     0x44444457, 0x4444444c, 0x44444458, 0x44444440, 0x4444444f, 0x44444446, 0x4444444d, 0x4444444b),
    (0x55574615, 0x55555574, 0x55555553, 0x55555540, 0x55555559, 0x5555547f, 0x55555561, 0x5555555c,
     0x5555555a, 0x55555552, 0x55555556, 0x5555555e, 0x5555555b, 0x55555557, 0x5555555d, 0x55555558),
    (0x66662806, 0x66666895, 0x66666684, 0x66666329, 0x66666973, 0x6666574c, 0x66666572, 0x6666687a,
     0x6666664b, 0x6666667d, 0x66666661, 0x66666668, 0x6666666e, 0x66666660, 0x66666667, 0x6666666f),
    (0x7779e3a7, 0x777777a5, 0x7777b459, 0x77777774, 0x77777596, 0x7777775b, 0x7777b8a3, 0x77777768,
     0x7777777c, 0x777777a2, 0x7777777e, 0x77778a91, 0x7777777f, 0x7777777a, 0x7777777d, 0x77777770),
    (0x8893b028, 0x8888c7a6, 0x88888889, 0x8888886b, 0x888888b5, 0x888888a4, 0x8888885d, 0x88888867,
     0x88888892, 0x88888883, 0x8888888c, 0x8888888a, 0x88888880, 0x8888888e, 0x8888888f, 0x88888881),
    (0x998a7169, 0x9999a78b, 0x9999996a, 0x99999a78, 0x99999987, 0x99999995, 0x999999bd, 0x99999990,
     0x999999c3, 0x9999999e, 0x99999996, 0x9999999c, 0x99999992, 0x99999991, 0x9999999f, 0x99999994),
    (0xaaac940a, 0xaaaaac09, 0xaaaaa86d, 0xaaaaaab7, 0xaaaaaacb, 0xaaaaa97e, 0xaaaaaaa8, 0xaaaaaaa6,
     0xaaaaa98c, 0xaaaaaaf5, 0xaaaaa870, 0xaaaaa98f, 0xaaaaa9b4, 0xaaaaaaa3, 0xaaaaaaa2, 0xaaaaaaa1),
    (0xbbbbb09b, 0xbbbbbbac, 0xbbbbbed8, 0xbbbbbbce, 0xbbbbbb60, 0xbbbbbdc7, 0xbbbbbbba, 0xbbbbbbb1,
     0xbbbbbbb9, 0xbbbbbbc5, 0xbbbbbbbf, 0xbbbbbbb2, 0xbbbbbbbd, 0xbbbbbbb6, 0xbbbbbbb3, 0xbbbbbbb4),
    (0xccccb16c, 0xccccc9ed, 0xccccc9b0, 0xcccccbda, 0xccccccbf, 0xccccccd9, 0xcccccc8e, 0xccccccb6,
     0xcccccccb, 0xccccccc7, 0xccccccc2, 0xccccccc8, 0xccccccc1, 0xccccccc4, 0xccccccc5, 0xccccccc3),
    (0xddddca0d, 0xdddddabe, 0xdddddea0, 0xddddddaf, 0xddddddea, 0xdddfecb2, 0xddddddc8, 0xdddddec1,
     0xddddddc4, 0xdddddde9, 0xddddddfc, 0xdddddde5, 0xddddddd7, 0xdddddddb, 0xddddddd6, 0xddddddd3),
    (0xeeeed1fe, 0xeeeeeedf, 0xeeeeeefd, 0xeeeeeef0, 0xeeeeeefb, 0xeeeeeee7, 0xeeeeeee4, 0xeeeeeef8,
     0xeeeeeeea, 0xeeeeeee2, 0xeeeeeed3, 0xeeeeeee1, 0xeeeeeee6, 0xeeeeeee9, 0xeeeeeeec, 0xeeeeeee5),
    (0xffff3e0f, 0xfffffffe, 0xfffffd01, 0xfffffed4, 0xffffffe3, 0xffffffe6, 0xfffffffd, 0xfffffff0,
     0xfffffffb, 0xfffffff2, 0xfffffff9, 0xfffffff8, 0xfffffff7, 0xfffffff5, 0xfffffffa, 0xfffffffc),
)

def signed(word):
    return word - (1 << 32) if word >= 1 << 31 else word


def by_z(z, values):
    picked = jnp.int32(signed(values[0]))
    for k in range(1, 16):
        if values[k] != values[0]:
            picked = jnp.where(z == k, jnp.int32(signed(values[k])), picked)
    return picked


def nibble(word, k):
    return (word >> (4 * k)) & 15


def quarter(word):
    first = (word & 15) // SPAN * SPAN
    return range(first, first + SPAN)


def targets(z):
    found = []
    for word in TREE[z]:
        for k in range(1, 8):
            d = (word >> (4 * k)) & 15
            if d != z and d not in found:
                found.append(d)
    return found


SENDS = [sum((word >> (4 * k)) & 15 != z for word in TREE[z] for k in range(1, 8)) for z in range(16)]
MOST = max(SENDS)
TARGETS = [len(targets(z)) for z in range(16)]
LAST = [
    sum(1 << k for k in range(16) if all(TREE[z][i] & 15 != q for i in range(k + 1, 16) for q in quarter(TREE[z][k])))
    for z in range(16)
]
GROUPS = tuple(q // SPAN for q in (0, 2, 4, 6, 14, 12, 10, 8)) if SPAN == 2 else (0, 1, 3, 2)
SOURCES = [sum(1 << z for z in range(16) if d in targets(z)) for d in range(16)]


def labels(position, base, occ, vir):
    first = base // NVIR
    orbital = jnp.full_like(position, first)
    for k in (1, 2):
        orbital += (position >= (first + k) * NVIR).astype(jnp.int32)
    virtual = position - orbital * NVIR
    occ_part = jnp.zeros_like(position)
    vir_part = jnp.zeros_like(position)
    occ_bound = jnp.int32(0)
    vir_bound = jnp.int32(0)
    for k in range(7):
        occ_bound += occ[k]
        vir_bound += vir[k]
        occ_part += (orbital >= occ_bound).astype(jnp.int32)
        vir_part += (virtual >= vir_bound).astype(jnp.int32)
    return occ_part ^ vir_part


def split(x):
    high = x.astype(BF16)
    return high, (x - high.astype(F32)).astype(BF16)


def product(left, right):
    dims = (((0,), (0,)), ((), ()))
    lh, ll = split(left)
    rh, rl = split(right)
    dot = lambda a, b: lax.dot_general(a, b, dims, preferred_element_type=F32)
    return dot(lh, rh) + (dot(lh, rl) + dot(ll, rh))


def kernel(
    a_hbm, b_hbm, occ_hbm, vir_hbm, o_ref,
    w, br, bc, ac, row_lab, occ, vir,
    local, w_in, br_in, bc_in, ac_in, cross_in, ready,
    tree_out, cross_out, br_out, bc_out, ac_out, pair_out,
):
    row = lax.axis_index("row")
    col = lax.axis_index("col")
    z = col % 16
    yhi = col // 16
    ylo = row // 8
    core = row % 2
    x = row // 2 % 4

    own = [
        pltpu.make_async_copy(a_hbm.at[:, pl.ds(256 * h, 256)], w.at[col, h], local.at[h])
        for h in (0, 1)
    ] + [
        pltpu.make_async_copy(b_hbm.at[pl.ds(8 * h, 8)], w.at[col, 2 + h], local.at[2 + h])
        for h in (0, 1)
    ]
    small = [
        pltpu.make_async_copy(occ_hbm, occ, local.at[4]),
        pltpu.make_async_copy(vir_hbm, vir, local.at[5]),
        pltpu.make_async_copy(b_hbm.at[pl.ds(0, 8)], bc.at[row, 0], local.at[6]),
        pltpu.make_async_copy(b_hbm.at[pl.ds(8, 8)], bc.at[row, 1], local.at[7]),
    ]
    for copy in own + small:
        copy.start()

    barrier = pltpu.get_barrier_semaphore()
    sources = by_z(z, SOURCES)

    def greet_z(d, carry):
        @pl.when(((sources >> d) & 1) == 1)
        def _():
            pl.semaphore_signal(
                barrier, inc=1, device_id={"row": row, "col": yhi * 16 + d}, device_id_type=MESH
            )
        return carry

    other = {"row": row + 1 - 2 * core, "col": col}
    peers = [other]
    peers += [{"row": ylo * 8 + (x + k) % 4 * 2 + core, "col": col} for k in (1, 2, 3)]
    peers += [
        {"row": (ylo + k % 2) % 2 * 8 + x * 2 + core, "col": (yhi + k // 2) % 2 * 16 + z} for k in (1, 2, 3)
    ]
    late = z >= 8

    @pl.when(late)
    def _():
        for peer in peers:
            pl.semaphore_signal(barrier, inc=1, device_id=peer, device_id_type=MESH)

    @pl.when(jnp.logical_not(late))
    def _():
        def greet_plane(t, carry):
            r, y = t % 16, t // 16

            @pl.when(jnp.logical_or(r != row, y != yhi))
            def _():
                pl.semaphore_signal(
                    barrier, inc=1, device_id={"row": r, "col": y * 16 + z}, device_id_type=MESH
                )
            return carry

        lax.fori_loop(0, 32, greet_plane, 0)

    lax.fori_loop(0, 16, greet_z, 0)

    pl.semaphore_wait(barrier, jnp.where(late, 7, 31) + by_z(z, TARGETS))

    @pl.when(late)
    def _():
        for peer in peers:
            pl.semaphore_signal(ready.at[0], inc=1, device_id=peer, device_id_type=MESH)

    for copy in own:
        copy.wait()

    def send_tree(s, d, j):
        c = yhi * 16 + s
        pltpu.make_async_remote_copy(
            src_ref=w.at[c], dst_ref=w.at[c], send_sem=tree_out.at[j], recv_sem=w_in.at[s],
            device_id={"row": row, "col": yhi * 16 + d}, device_id_type=MESH,
        ).start()

    def cross(s):
        c = yhi * 16 + s
        return pltpu.make_async_remote_copy(
            src_ref=w.at[c, pl.ds(0, 2)], dst_ref=w.at[c, pl.ds(0, 2)], send_sem=cross_out,
            recv_sem=cross_in, device_id={"row": row, "col": (1 - yhi) * 16 + z}, device_id_type=MESH,
        )

    def to_rows(s, y):
        r = yhi * 8 + s // 2
        source = w.at[yhi * 16 + s, pl.ds(2, 2)]
        me = jnp.logical_and(r == row, y == yhi)

        @pl.when(me)
        def _():
            pltpu.make_async_copy(source, br.at[row, s % 2], br_in).start()

        @pl.when(jnp.logical_not(me))
        def _():
            pltpu.make_async_remote_copy(
                src_ref=source, dst_ref=br.at[row, s % 2], send_sem=br_out, recv_sem=br_in,
                device_id={"row": r, "col": y * 16 + z}, device_id_type=MESH,
            ).start()

    owner = row % 8 == z // 2
    half = z % 2

    def to_plane(g):
        c = yhi * 16 + SPAN * g
        t = yhi * (16 // SPAN) + g
        source = w.at[pl.ds(c, SPAN), half]

        def one(chip, carry):
            r = 2 * chip + core
            me = jnp.logical_and(r == row, ylo == yhi)

            @pl.when(me)
            def _():
                pltpu.make_async_copy(source, ac.at[pl.ds(c, SPAN)], ac_in.at[t]).start()

            @pl.when(jnp.logical_not(me))
            def _():
                pltpu.make_async_remote_copy(
                    src_ref=source, dst_ref=ac.at[pl.ds(c, SPAN)], send_sem=ac_out.at[g],
                    recv_sem=ac_in.at[t],
                    device_id={"row": r, "col": ylo * 16 + z}, device_id_type=MESH,
                ).start()
            return carry

        lax.fori_loop(0, 8, one, 0)

    last = by_z(z, LAST)
    sent = jnp.int32(0)
    for k in range(16):
        word = by_z(z, [TREE[v][k] for v in range(16)])
        s = nibble(word, 0)
        if k:
            pltpu.make_async_copy(w.at[s], w.at[s], w_in.at[s]).wait()

        def forward(i, j):
            d = (word >> (4 * i)) & 15
            there = d != z

            @pl.when(there)
            def _():
                send_tree(s, d, j)
            return j + there.astype(jnp.int32)

        sent = lax.fori_loop(1, 8, forward, sent)
        if k == 0:
            @pl.when(late)
            def _():
                pl.semaphore_wait(ready.at[0], 7)
                pl.semaphore_signal(ready.at[1], inc=1, device_id=other, device_id_type=MESH)
                pl.semaphore_wait(ready.at[1], 1)
        cross(s).start()
        to_rows(s, 0)
        to_rows(s, 1)

        @pl.when(jnp.logical_and(owner, ((last >> k) & 1) == 1))
        def _():
            to_plane(s // SPAN)

        if k == 0:
            def give(r, carry):
                @pl.when(r != row)
                def _():
                    pltpu.make_async_remote_copy(
                        src_ref=w.at[col, pl.ds(2, 2)], dst_ref=bc.at[row], send_sem=bc_out,
                        recv_sem=bc_in, device_id={"row": r, "col": col}, device_id_type=MESH,
                    ).start()
                return carry

            lax.fori_loop(0, 16, give, 0)
            for copy in small:
                copy.wait()
            row_pos = row * 512 + lax.broadcasted_iota(jnp.int32, (512, 128), 0)
            row_lab[...] = labels(row_pos, row * 512, occ, vir)

    first = core == (z // 2) % 2

    def group(t):
        return ac.at[pl.ds(SPAN * t, SPAN)]

    @pl.when(first)
    def _():
        for g in GROUPS:
            for y in (0, 1):
                t = 16 // SPAN * y + g
                pltpu.make_async_copy(group(t), group(t), ac_in.at[t]).wait()
                pltpu.make_async_remote_copy(
                    src_ref=group(t), dst_ref=group(t), send_sem=pair_out.at[t],
                    recv_sem=ac_in.at[t], device_id={"row": 2 * (row // 2) + 1 - core, "col": col},
                    device_id_type=MESH,
                ).start()

    pltpu.make_async_copy(bc.at[pl.ds(0, 15)], bc.at[pl.ds(0, 15)], bc_in).wait()
    pltpu.make_async_copy(ac, ac, cross_in).wait()
    pltpu.make_async_copy(br, br, br_in).wait()

    @pl.when(jnp.logical_not(first))
    def _():
        for t in range(32 // SPAN):
            pltpu.make_async_copy(group(t), group(t), ac_in.at[t]).wait()

    col_lab = labels(
        col * 256 + lax.broadcasted_iota(jnp.int32, (8, 256), 1), col * 256, occ, vir
    )[:1]
    b_here = bc[...].reshape(256, 256)
    a_here = ac[...].reshape(256, 256)
    for m in (0, 1):
        rows = slice(256 * m, 256 * (m + 1))
        total = product(w[:, m].reshape(256, 256), b_here) + product(br[:, m].reshape(256, 256), a_here)
        lab = row_lab[rows]
        for h in (0, 1):
            lanes = slice(128 * h, 128 * (h + 1))
            o_ref[rows, lanes] = jnp.where(lab == col_lab[:, lanes], total[:, lanes], 0.0)

    def sent_tree(j, carry):
        pltpu.make_async_copy(w.at[0], w.at[0], tree_out.at[j]).wait()
        return carry

    lax.fori_loop(0, by_z(z, SENDS), sent_tree, 0)
    pltpu.make_async_copy(ac, ac, cross_out).wait()
    pltpu.make_async_copy(bc.at[pl.ds(0, 15)], bc.at[pl.ds(0, 15)], bc_out).wait()

    @pl.when(ylo == yhi)
    def _():
        pltpu.make_async_copy(br.at[pl.ds(0, 15)], br.at[pl.ds(0, 15)], br_out).wait()

    @pl.when(ylo != yhi)
    def _():
        pltpu.make_async_copy(br, br, br_out).wait()

    @pl.when(owner)
    def _():
        for g in range(16 // SPAN):
            @pl.when(ylo == yhi)
            def _():
                pltpu.make_async_copy(ac.at[pl.ds(0, 7 * SPAN)], ac.at[pl.ds(0, 7 * SPAN)], ac_out.at[g]).wait()

            @pl.when(ylo != yhi)
            def _():
                pltpu.make_async_copy(ac.at[pl.ds(0, 8 * SPAN)], ac.at[pl.ds(0, 8 * SPAN)], ac_out.at[g]).wait()

    @pl.when(first)
    def _():
        for t in range(32 // SPAN):
            pltpu.make_async_copy(group(t), group(t), pair_out.at[t]).wait()


def per_device(amplitudes, integrals, occ_counts, vir_counts):
    arrays = (amplitudes.T, integrals, occ_counts, vir_counts)
    hbm = pl.BlockSpec(memory_space=pltpu.HBM)
    dma = pltpu.SemaphoreType.DMA
    return pl.pallas_call(
        kernel,
        out_shape=jax.ShapeDtypeStruct((512, 256), F32),
        in_specs=[hbm, hbm, hbm, hbm],
        out_specs=pl.BlockSpec(memory_space=pltpu.VMEM),
        scratch_shapes=[
            pltpu.VMEM((32, 4, 8, 256), F32),
            pltpu.VMEM((16, 2, 2, 8, 256), F32),
            pltpu.VMEM((16, 2, 8, 256), F32),
            pltpu.VMEM((32, 8, 256), F32),
            pltpu.VMEM((512, 128), jnp.int32),
            pltpu.SMEM((8,), jnp.int32),
            pltpu.SMEM((8,), jnp.int32),
            dma((8,)), dma((16,)), dma, dma, dma((32 // SPAN,)), dma,
            pltpu.SemaphoreType.REGULAR((2,)),
            dma((MOST,)), dma, dma, dma, dma((16 // SPAN,)), dma((32 // SPAN,)),
        ],
        compiler_params=pltpu.CompilerParams(
            collective_id=0, has_side_effects=True, vmem_limit_bytes=32 * 2**20
        ),
    )(*[pltpu.with_memory_space_constraint(v, pltpu.HBM) for v in arrays])


def solution(mesh):
    placed = (P("row", "col"), P("row", "col"), P(), P())
    return jax.shard_map(
        per_device, mesh=mesh, in_specs=placed, out_specs=P("row", "col"), check_vma=False
    )
```

```python
import jax
import jax.numpy as jnp
from jax import lax
from jax.experimental import pallas as pl
from jax.experimental.pallas import tpu as pltpu
from jax.sharding import PartitionSpec as P

NVIR = 400
SPAN = 2
SHARE_AFTER = 13
MESH = pl.DeviceIdType.MESH
F32 = jnp.float32
BF16 = jnp.bfloat16

TREE = (
    (0x002fd1e0, 0x000000f4, 0x000000c1, 0x0000001f, 0x000000e3, 0x0000013e, 0x000000f5, 0x00000df2,
     0x00000e1b, 0x00000d19, 0x0000003c, 0x00000fed, 0x00000007, 0x0000000a, 0x000000d8, 0x00000ef6),
    (0x11142f01, 0x11111032, 0x11111113, 0x11111130, 0x11111114, 0x11111115, 0x1111120d, 0x11111107,
     0x1111111f, 0x1111203a, 0x1111112e, 0x1111123b, 0x111111fc, 0x11111119, 0x111111f8, 0x11111116),
    (0x22226412, 0x22222224, 0x22222361, 0x22222223, 0x22222240, 0x22222347, 0x2222222f, 0x22222225,
     0x22222208, 0x2222243d, 0x22222229, 0x2222222a, 0x22222246, 0x2222222e, 0x2222222c, 0x2222222b),
    (0x33264013, 0x33333614, 0x33333425, 0x3333364f, 0x33333351, 0x33333332, 0x33351206, 0x33333350,
     0x33333338, 0x3333345e, 0x33333339, 0x33333337, 0x3333333a, 0x3333333d, 0x3333333c, 0x3333333b),
    (0x44430254, 0x44444453, 0x44444452, 0x44444441, 0x44443529, 0x44444445, 0x4444445f, 0x44444440,
     0x4444444a, 0x44444447, 0x4444444b, 0x4444444c, 0x4444444e, 0x4444444d, 0x44444448, 0x44444446),
    (0x55613705, 0x55555574, 0x55555553, 0x55555572, 0x5555547b, 0x5555524c, 0x55555769, 0x55555571,
     0x55555558, 0x5555555f, 0x55555556, 0x55555760, 0x5555555d, 0x5555555e, 0x55555557, 0x5555555a),
    (0x66666736, 0x66666665, 0x66667d93, 0x66666692, 0x66666664, 0x66666661, 0x6666666d, 0x66666648,
     0x6666667f, 0x66666657, 0x6666665a, 0x666666e9, 0x6666666c, 0x6666666b, 0x66666660, 0x6666666e),
    (0x77728917, 0x77777985, 0x77777784, 0x77777568, 0x77777786, 0x77777783, 0x77777772, 0x7777776c,
     0x7777768b, 0x7777779e, 0x7777777d, 0x7777778f, 0x77777779, 0x77777771, 0x7777777a, 0x77777770),
    (0x8897c328, 0x8888884a, 0x88888887, 0x888888b5, 0x88888894, 0x88888889, 0x8889bcd6, 0x88888883,
     0x8888888c, 0x8888888d, 0x88888882, 0x8888888b, 0x8888888f, 0x88888880, 0x88888881, 0x8888888e),
    (0x999c0a49, 0x99996ca7, 0x99999b6a, 0x999999ab, 0x99999998, 0x999999c5, 0x999999a3, 0x9999997d,
     0x99999994, 0x99999982, 0x9999999c, 0x999999cf, 0x999999a6, 0x9999998e, 0x99999990, 0x99999991),
    (0xaaac198a, 0xaaaaaa89, 0xaaaaaaa7, 0xaaaaa98c, 0xaaaaaa8d, 0xaaaaaacb, 0xaaaaaa6e, 0xaaaaabc3,
     0xaaaaa890, 0xaaaaaaa8, 0xaaaaa891, 0xaaaaaac4, 0xaaaaaaa5, 0xaaaaaaaf, 0xaaaaaaa6, 0xaaaaaaa2),
    (0xbbbb509b, 0xbbbbba7c, 0xbbbb5a9d, 0xbbbbbb7e, 0xbbbbbd9f, 0xbbbbbb7a, 0xbbbbbac0, 0xbbbbbae8,
     0xbbbbbbd5, 0xbbbbbbb7, 0xbbbbbbb1, 0xbbbbbbb4, 0xbbbbbbb3, 0xbbbbbba2, 0xbbbbbbb6, 0xbbbbbbb9),
    (0xcccc5bdc, 0xccccceda, 0xcccccccd, 0xccccccf9, 0xcccccb18, 0xcccccafe, 0xccccdeb7, 0xcccccda1,
     0xcccccae5, 0xccccccc0, 0xcccccccb, 0xccccccc2, 0xccccccc6, 0xccccccc3, 0xcccccccf, 0xccccccc4),
    (0xdddc16bd, 0xddddd10c, 0xddddddce, 0xddddddb0, 0xddddddfa, 0xdddddba4, 0xddddebc2, 0xddddddaf,
     0xddddddb9, 0xddddddf7, 0xddddddd1, 0xddddddf3, 0xdddddddb, 0xddddddd8, 0xddddddd5, 0xddddddd6),
    (0xeeeedb0e, 0xeeeeeebf, 0xeeeeeee0, 0xeeeeeee3, 0xeeeeeeb1, 0xeeeeeeea, 0xeeeeeee4, 0xeeeeedfb,
     0xeeeeeee7, 0xeeeeeeed, 0xeeeeeee2, 0xeeeeeee8, 0xeeeeeee5, 0xeeeeeee6, 0xeeeeeeec, 0xeeeeeee9),
    (0xfff20e3f, 0xfffffff0, 0xffffffe1, 0xfffffed4, 0xfffffff5, 0xfffffff2, 0xfffffff9, 0xfffffffa,
     0xfffffffe, 0xfffffffd, 0xffffffec, 0xfffffffb, 0xfffffff6, 0xfffffff8, 0xfffffff7, 0xfffffff3),
)

def signed(word):
    return word - (1 << 32) if word >= 1 << 31 else word


def by_z(z, values):
    picked = jnp.int32(signed(values[0]))
    for k in range(1, 16):
        if values[k] != values[0]:
            picked = jnp.where(z == k, jnp.int32(signed(values[k])), picked)
    return picked


def nibble(word, k):
    return (word >> (4 * k)) & 15


def quarter(word):
    first = (word & 15) // SPAN * SPAN
    return range(first, first + SPAN)


def targets(z):
    found = []
    for word in TREE[z]:
        for k in range(1, 8):
            d = (word >> (4 * k)) & 15
            if d != z and d not in found:
                found.append(d)
    return found


SENDS = [sum((word >> (4 * k)) & 15 != z for word in TREE[z] for k in range(1, 8)) for z in range(16)]
MOST = max(SENDS)
TARGETS = [len(targets(z)) for z in range(16)]
LAST = [
    sum(1 << k for k in range(16) if all(TREE[z][i] & 15 != q for i in range(k + 1, 16) for q in quarter(TREE[z][k])))
    for z in range(16)
]
GROUPS = tuple(q // SPAN for q in (0, 2, 4, 6, 14, 12, 10, 8)) if SPAN == 2 else (0, 1, 3, 2)
SOURCES = [sum(1 << z for z in range(16) if d in targets(z)) for d in range(16)]


def labels(position, base, occ, vir):
    first = base // NVIR
    orbital = jnp.full_like(position, first)
    for k in (1, 2):
        orbital += (position >= (first + k) * NVIR).astype(jnp.int32)
    virtual = position - orbital * NVIR
    occ_part = jnp.zeros_like(position)
    vir_part = jnp.zeros_like(position)
    occ_bound = jnp.int32(0)
    vir_bound = jnp.int32(0)
    for k in range(7):
        occ_bound += occ[k]
        vir_bound += vir[k]
        occ_part += (orbital >= occ_bound).astype(jnp.int32)
        vir_part += (virtual >= vir_bound).astype(jnp.int32)
    return occ_part ^ vir_part


def split(x):
    high = x.astype(BF16)
    return high, (x - high.astype(F32)).astype(BF16)


def product(left, right):
    dims = (((0,), (0,)), ((), ()))
    lh, ll = split(left)
    rh, rl = split(right)
    dot = lambda a, b: lax.dot_general(a, b, dims, preferred_element_type=F32)
    return dot(lh, rh) + (dot(lh, rl) + dot(ll, rh))


def kernel(
    a_hbm, b_hbm, occ_hbm, vir_hbm, o_ref,
    w, br, bc, ac, row_lab, occ, vir,
    local, w_in, br_in, bc_in, ac_in, cross_in, ap_in, share_in, ready,
    tree_out, cross_out, br_out, bc_out, ac_out, pair_out, ap_out, share_out,
):
    row = lax.axis_index("row")
    col = lax.axis_index("col")
    z = col % 16
    yhi = col // 16
    ylo = row // 8
    core = row % 2
    x = row // 2 % 4

    own = [
        pltpu.make_async_copy(a_hbm.at[:, pl.ds(256 * h, 256)], w.at[col, h], local.at[h])
        for h in (0, 1)
    ] + [
        pltpu.make_async_copy(b_hbm.at[pl.ds(8 * h, 8)], w.at[col, 2 + h], local.at[2 + h])
        for h in (0, 1)
    ]
    small = [
        pltpu.make_async_copy(occ_hbm, occ, local.at[4]),
        pltpu.make_async_copy(vir_hbm, vir, local.at[5]),
        pltpu.make_async_copy(b_hbm.at[pl.ds(0, 8)], bc.at[row, 0], local.at[6]),
        pltpu.make_async_copy(b_hbm.at[pl.ds(8, 8)], bc.at[row, 1], local.at[7]),
    ]
    for copy in own + small:
        copy.start()

    barrier = pltpu.get_barrier_semaphore()
    sources = by_z(z, SOURCES)

    def greet_z(d, carry):
        @pl.when(((sources >> d) & 1) == 1)
        def _():
            pl.semaphore_signal(
                barrier, inc=1, device_id={"row": row, "col": yhi * 16 + d}, device_id_type=MESH
            )
        return carry

    other = {"row": row + 1 - 2 * core, "col": col}
    peers = [other]
    peers += [{"row": ylo * 8 + (x + k) % 4 * 2 + core, "col": col} for k in (1, 2, 3)]
    peers += [
        {"row": (ylo + k % 2) % 2 * 8 + x * 2 + core, "col": (yhi + k // 2) % 2 * 16 + z} for k in (1, 2, 3)
    ]
    late = z >= 8

    @pl.when(late)
    def _():
        for peer in peers:
            pl.semaphore_signal(barrier, inc=1, device_id=peer, device_id_type=MESH)

    @pl.when(jnp.logical_not(late))
    def _():
        def greet_plane(t, carry):
            r, y = t % 16, t // 16

            @pl.when(jnp.logical_or(r != row, y != yhi))
            def _():
                pl.semaphore_signal(
                    barrier, inc=1, device_id={"row": r, "col": y * 16 + z}, device_id_type=MESH
                )
            return carry

        lax.fori_loop(0, 32, greet_plane, 0)

    lax.fori_loop(0, 16, greet_z, 0)

    share = ylo * 8 + (x - z // 4 + 6) % 4 * 2 + core
    early = jnp.logical_not(late)
    shares = jnp.logical_and(early, share % 8 >= 4)
    direct = jnp.logical_and(late, x < 2)

    @pl.when(shares)
    def _():
        for e in (0, 1):
            pl.semaphore_signal(
                barrier, inc=1, device_id={"row": col // 2, "col": 2 * share + e}, device_id_type=MESH
            )

    pl.semaphore_wait(
        barrier, jnp.where(late, 7, 31) + by_z(z, TARGETS) + 2 * direct.astype(jnp.int32)
    )

    @pl.when(late)
    def _():
        for peer in peers:
            pl.semaphore_signal(ready.at[0], inc=1, device_id=peer, device_id_type=MESH)

    for copy in own:
        copy.wait()

    def send_tree(s, d, j):
        c = yhi * 16 + s
        pltpu.make_async_remote_copy(
            src_ref=w.at[c], dst_ref=w.at[c], send_sem=tree_out.at[j], recv_sem=w_in.at[s],
            device_id={"row": row, "col": yhi * 16 + d}, device_id_type=MESH,
        ).start()

    def cross(s):
        c = yhi * 16 + s
        return pltpu.make_async_remote_copy(
            src_ref=w.at[c, pl.ds(0, 2)], dst_ref=w.at[c, pl.ds(0, 2)], send_sem=cross_out,
            recv_sem=cross_in, device_id={"row": row, "col": (1 - yhi) * 16 + z}, device_id_type=MESH,
        )

    def to_rows(s, y):
        r = yhi * 8 + s // 2
        source = w.at[yhi * 16 + s, pl.ds(2, 2)]
        me = jnp.logical_and(r == row, y == yhi)

        @pl.when(me)
        def _():
            pltpu.make_async_copy(source, br.at[row, s % 2], br_in).start()

        @pl.when(jnp.logical_not(me))
        def _():
            pltpu.make_async_remote_copy(
                src_ref=source, dst_ref=br.at[row, s % 2], send_sem=br_out, recv_sem=br_in,
                device_id={"row": r, "col": y * 16 + z}, device_id_type=MESH,
            ).start()

    owner = row % 8 == z // 2
    half = z % 2

    def to_plane(g):
        c = yhi * 16 + SPAN * g
        t = yhi * (16 // SPAN) + g
        source = w.at[pl.ds(c, SPAN), half]

        def one(chip, carry):
            r = 2 * chip + core
            me = jnp.logical_and(r == row, ylo == yhi)

            @pl.when(me)
            def _():
                pltpu.make_async_copy(source, ac.at[pl.ds(c, SPAN)], ac_in.at[t]).start()

            @pl.when(jnp.logical_not(me))
            def _():
                pltpu.make_async_remote_copy(
                    src_ref=source, dst_ref=ac.at[pl.ds(c, SPAN)], send_sem=ac_out.at[g],
                    recv_sem=ac_in.at[t],
                    device_id={"row": r, "col": ylo * 16 + z}, device_id_type=MESH,
                ).start()
            return carry

        lax.fori_loop(0, 8, one, 0)

    def direct_to(h):
        r = yhi * 8 + (x + z // 4 + 2) % 4 * 2 + z // 2 % 2
        return pltpu.make_async_remote_copy(
            src_ref=w.at[col, h], dst_ref=ac.at[col], send_sem=ap_out.at[h], recv_sem=ap_in,
            device_id={"row": r, "col": 2 * row + h}, device_id_type=MESH,
        )

    share_piece = ac.at[pl.ds(2 * share, 2)]

    last = by_z(z, LAST)
    sent = jnp.int32(0)
    for k in range(16):
        word = by_z(z, [TREE[v][k] for v in range(16)])
        s = nibble(word, 0)
        if k:
            pltpu.make_async_copy(w.at[s], w.at[s], w_in.at[s]).wait()

        def forward(i, j):
            d = (word >> (4 * i)) & 15
            there = d != z

            @pl.when(there)
            def _():
                send_tree(s, d, j)
            return j + there.astype(jnp.int32)

        sent = lax.fori_loop(1, 8, forward, sent)
        if k == 0:
            @pl.when(direct)
            def _():
                direct_to(0).start()
                direct_to(1).start()

            @pl.when(late)
            def _():
                pl.semaphore_wait(ready.at[0], 7)
                pl.semaphore_signal(ready.at[1], inc=1, device_id=other, device_id_type=MESH)
                pl.semaphore_wait(ready.at[1], 1)
        cross(s).start()
        to_rows(s, 0)
        to_rows(s, 1)

        @pl.when(
            jnp.logical_and(jnp.logical_and(owner, ((last >> k) & 1) == 1), jnp.logical_or(late, s < 8))
        )
        def _():
            to_plane(s // SPAN)

        if k == 0:
            def give(r, carry):
                @pl.when(r != row)
                def _():
                    pltpu.make_async_remote_copy(
                        src_ref=w.at[col, pl.ds(2, 2)], dst_ref=bc.at[row], send_sem=bc_out,
                        recv_sem=bc_in, device_id={"row": r, "col": col}, device_id_type=MESH,
                    ).start()
                return carry

            lax.fori_loop(0, 16, give, 0)
            for copy in small:
                copy.wait()
            row_pos = row * 512 + lax.broadcasted_iota(jnp.int32, (512, 128), 0)
            row_lab[...] = labels(row_pos, row * 512, occ, vir)

        if k == SHARE_AFTER:
            @pl.when(shares)
            def _():
                pltpu.make_async_copy(share_piece, share_piece, ap_in).wait()

                def give_share(r, carry):
                    @pl.when(r != row)
                    def _():
                        pltpu.make_async_remote_copy(
                            src_ref=share_piece, dst_ref=share_piece, send_sem=share_out,
                            recv_sem=share_in, device_id={"row": r, "col": col}, device_id_type=MESH,
                        ).start()
                    return carry

                lax.fori_loop(0, 16, give_share, 0)

    first = core == (z // 2) % 2

    def group(t):
        return ac.at[pl.ds(SPAN * t, SPAN)]

    for g in GROUPS:
        @pl.when(jnp.logical_and(first, late) if g * SPAN >= 8 else first)
        def _():
            for y in (0, 1):
                t = 16 // SPAN * y + g
                pltpu.make_async_copy(group(t), group(t), ac_in.at[t]).wait()
                pltpu.make_async_remote_copy(
                    src_ref=group(t), dst_ref=group(t), send_sem=pair_out.at[t],
                    recv_sem=ac_in.at[t], device_id={"row": 2 * (row // 2) + 1 - core, "col": col},
                    device_id_type=MESH,
                ).start()

    pltpu.make_async_copy(bc.at[pl.ds(0, 15)], bc.at[pl.ds(0, 15)], bc_in).wait()
    pltpu.make_async_copy(ac, ac, cross_in).wait()
    b_here = bc[...].reshape(256, 256)
    for m in (0, 1):
        o_ref[256 * m : 256 * (m + 1)] = product(w[:, m].reshape(256, 256), b_here)

    pltpu.make_async_copy(br, br, br_in).wait()

    for t in range(32 // SPAN):
        here = jnp.logical_not(first)

        @pl.when(jnp.logical_and(here, late) if t * SPAN % 16 >= 8 else here)
        def _():
            pltpu.make_async_copy(group(t), group(t), ac_in.at[t]).wait()

    @pl.when(shares)
    def _():
        pltpu.make_async_copy(ac.at[pl.ds(0, 14)], ac.at[pl.ds(0, 14)], share_in).wait()

    @pl.when(jnp.logical_and(early, jnp.logical_not(shares)))
    def _():
        pltpu.make_async_copy(ac.at[pl.ds(0, 16)], ac.at[pl.ds(0, 16)], share_in).wait()

    col_lab = labels(
        col * 256 + lax.broadcasted_iota(jnp.int32, (8, 256), 1), col * 256, occ, vir
    )[:1]
    a_here = ac[...].reshape(256, 256)
    for m in (0, 1):
        rows = slice(256 * m, 256 * (m + 1))
        total = o_ref[rows] + product(br[:, m].reshape(256, 256), a_here)
        lab = row_lab[rows]
        for h in (0, 1):
            lanes = slice(128 * h, 128 * (h + 1))
            o_ref[rows, lanes] = jnp.where(lab == col_lab[:, lanes], total[:, lanes], 0.0)

    def sent_tree(j, carry):
        pltpu.make_async_copy(w.at[0], w.at[0], tree_out.at[j]).wait()
        return carry

    lax.fori_loop(0, by_z(z, SENDS), sent_tree, 0)
    pltpu.make_async_copy(ac, ac, cross_out).wait()
    pltpu.make_async_copy(bc.at[pl.ds(0, 15)], bc.at[pl.ds(0, 15)], bc_out).wait()

    @pl.when(ylo == yhi)
    def _():
        pltpu.make_async_copy(br.at[pl.ds(0, 15)], br.at[pl.ds(0, 15)], br_out).wait()

    @pl.when(ylo != yhi)
    def _():
        pltpu.make_async_copy(br, br, br_out).wait()

    for g in range(16 // SPAN):
        gave = jnp.logical_and(owner, late) if g * SPAN >= 8 else owner

        @pl.when(jnp.logical_and(gave, ylo == yhi))
        def _():
            pltpu.make_async_copy(ac.at[pl.ds(0, 7 * SPAN)], ac.at[pl.ds(0, 7 * SPAN)], ac_out.at[g]).wait()

        @pl.when(jnp.logical_and(gave, ylo != yhi))
        def _():
            pltpu.make_async_copy(ac.at[pl.ds(0, 8 * SPAN)], ac.at[pl.ds(0, 8 * SPAN)], ac_out.at[g]).wait()

    for t in range(32 // SPAN):
        @pl.when(jnp.logical_and(first, late) if t * SPAN % 16 >= 8 else first)
        def _():
            pltpu.make_async_copy(group(t), group(t), pair_out.at[t]).wait()

    @pl.when(direct)
    def _():
        direct_to(0).wait_send()
        direct_to(1).wait_send()

    @pl.when(shares)
    def _():
        pltpu.make_async_copy(ac.at[pl.ds(0, 30)], ac.at[pl.ds(0, 30)], share_out).wait()


def per_device(amplitudes, integrals, occ_counts, vir_counts):
    arrays = (amplitudes.T, integrals, occ_counts, vir_counts)
    hbm = pl.BlockSpec(memory_space=pltpu.HBM)
    dma = pltpu.SemaphoreType.DMA
    return pl.pallas_call(
        kernel,
        out_shape=jax.ShapeDtypeStruct((512, 256), F32),
        in_specs=[hbm, hbm, hbm, hbm],
        out_specs=pl.BlockSpec(memory_space=pltpu.VMEM),
        scratch_shapes=[
            pltpu.VMEM((32, 4, 8, 256), F32),
            pltpu.VMEM((16, 2, 2, 8, 256), F32),
            pltpu.VMEM((16, 2, 8, 256), F32),
            pltpu.VMEM((32, 8, 256), F32),
            pltpu.VMEM((512, 128), jnp.int32),
            pltpu.SMEM((8,), jnp.int32),
            pltpu.SMEM((8,), jnp.int32),
            dma((8,)), dma((16,)), dma, dma, dma((32 // SPAN,)), dma,
            dma, dma, pltpu.SemaphoreType.REGULAR((2,)),
            dma((MOST,)), dma, dma, dma, dma((16 // SPAN,)), dma((32 // SPAN,)), dma((2,)), dma,
        ],
        compiler_params=pltpu.CompilerParams(
            collective_id=0, has_side_effects=True, vmem_limit_bytes=32 * 2**20
        ),
    )(*[pltpu.with_memory_space_constraint(v, pltpu.HBM) for v in arrays])


def solution(mesh):
    placed = (P("row", "col"), P("row", "col"), P(), P())
    return jax.shard_map(
        per_device, mesh=mesh, in_specs=placed, out_specs=P("row", "col"), check_vma=False
    )
```

```python
import jax
import jax.numpy as jnp
from jax import lax
from jax.experimental import pallas as pl
from jax.experimental.pallas import tpu as pltpu
from jax.sharding import PartitionSpec as P

NVIR = 400
SPAN = 2
SHARE_AFTER = 10
MESH = pl.DeviceIdType.MESH
F32 = jnp.float32
BF16 = jnp.bfloat16

TREE = (
    (0x002fd1e0, 0x000000f4, 0x000000c1, 0x0000001f, 0x000000e3, 0x0000013e, 0x000000f5, 0x00000df2,
     0x00000e1b, 0x00000d19, 0x0000003c, 0x00000fed, 0x00000007, 0x0000000a, 0x000000d8, 0x00000ef6),
    (0x11142f01, 0x11111032, 0x11111113, 0x11111130, 0x11111114, 0x11111115, 0x1111120d, 0x11111107,
     0x1111111f, 0x1111203a, 0x1111112e, 0x1111123b, 0x111111fc, 0x11111119, 0x111111f8, 0x11111116),
    (0x22226412, 0x22222224, 0x22222361, 0x22222223, 0x22222240, 0x22222347, 0x2222222f, 0x22222225,
     0x22222208, 0x2222243d, 0x22222229, 0x2222222a, 0x22222246, 0x2222222e, 0x2222222c, 0x2222222b),
    (0x33264013, 0x33333614, 0x33333425, 0x3333364f, 0x33333351, 0x33333332, 0x33351206, 0x33333350,
     0x33333338, 0x3333345e, 0x33333339, 0x33333337, 0x3333333a, 0x3333333d, 0x3333333c, 0x3333333b),
    (0x44430254, 0x44444453, 0x44444452, 0x44444441, 0x44443529, 0x44444445, 0x4444445f, 0x44444440,
     0x4444444a, 0x44444447, 0x4444444b, 0x4444444c, 0x4444444e, 0x4444444d, 0x44444448, 0x44444446),
    (0x55613705, 0x55555574, 0x55555553, 0x55555572, 0x5555547b, 0x5555524c, 0x55555769, 0x55555571,
     0x55555558, 0x5555555f, 0x55555556, 0x55555760, 0x5555555d, 0x5555555e, 0x55555557, 0x5555555a),
    (0x66666736, 0x66666665, 0x66667d93, 0x66666692, 0x66666664, 0x66666661, 0x6666666d, 0x66666648,
     0x6666667f, 0x66666657, 0x6666665a, 0x666666e9, 0x6666666c, 0x6666666b, 0x66666660, 0x6666666e),
    (0x77728917, 0x77777985, 0x77777784, 0x77777568, 0x77777786, 0x77777783, 0x77777772, 0x7777776c,
     0x7777768b, 0x7777779e, 0x7777777d, 0x7777778f, 0x77777779, 0x77777771, 0x7777777a, 0x77777770),
    (0x8897c328, 0x8888884a, 0x88888887, 0x888888b5, 0x88888894, 0x88888889, 0x8889bcd6, 0x88888883,
     0x8888888c, 0x8888888d, 0x88888882, 0x8888888b, 0x8888888f, 0x88888880, 0x88888881, 0x8888888e),
    (0x999c0a49, 0x99996ca7, 0x99999b6a, 0x999999ab, 0x99999998, 0x999999c5, 0x999999a3, 0x9999997d,
     0x99999994, 0x99999982, 0x9999999c, 0x999999cf, 0x999999a6, 0x9999998e, 0x99999990, 0x99999991),
    (0xaaac198a, 0xaaaaaa89, 0xaaaaaaa7, 0xaaaaa98c, 0xaaaaaa8d, 0xaaaaaacb, 0xaaaaaa6e, 0xaaaaabc3,
     0xaaaaa890, 0xaaaaaaa8, 0xaaaaa891, 0xaaaaaac4, 0xaaaaaaa5, 0xaaaaaaaf, 0xaaaaaaa6, 0xaaaaaaa2),
    (0xbbbb509b, 0xbbbbba7c, 0xbbbb5a9d, 0xbbbbbb7e, 0xbbbbbd9f, 0xbbbbbb7a, 0xbbbbbac0, 0xbbbbbae8,
     0xbbbbbbd5, 0xbbbbbbb7, 0xbbbbbbb1, 0xbbbbbbb4, 0xbbbbbbb3, 0xbbbbbba2, 0xbbbbbbb6, 0xbbbbbbb9),
    (0xcccc5bdc, 0xccccceda, 0xcccccccd, 0xccccccf9, 0xcccccb18, 0xcccccafe, 0xccccdeb7, 0xcccccda1,
     0xcccccae5, 0xccccccc0, 0xcccccccb, 0xccccccc2, 0xccccccc6, 0xccccccc3, 0xcccccccf, 0xccccccc4),
    (0xdddc16bd, 0xddddd10c, 0xddddddce, 0xddddddb0, 0xddddddfa, 0xdddddba4, 0xddddebc2, 0xddddddaf,
     0xddddddb9, 0xddddddf7, 0xddddddd1, 0xddddddf3, 0xdddddddb, 0xddddddd8, 0xddddddd5, 0xddddddd6),
    (0xeeeedb0e, 0xeeeeeebf, 0xeeeeeee0, 0xeeeeeee3, 0xeeeeeeb1, 0xeeeeeeea, 0xeeeeeee4, 0xeeeeedfb,
     0xeeeeeee7, 0xeeeeeeed, 0xeeeeeee2, 0xeeeeeee8, 0xeeeeeee5, 0xeeeeeee6, 0xeeeeeeec, 0xeeeeeee9),
    (0xfff20e3f, 0xfffffff0, 0xffffffe1, 0xfffffed4, 0xfffffff5, 0xfffffff2, 0xfffffff9, 0xfffffffa,
     0xfffffffe, 0xfffffffd, 0xffffffec, 0xfffffffb, 0xfffffff6, 0xfffffff8, 0xfffffff7, 0xfffffff3),
)

def signed(word):
    return word - (1 << 32) if word >= 1 << 31 else word


def by_z(z, values):
    picked = jnp.int32(signed(values[0]))
    for k in range(1, 16):
        if values[k] != values[0]:
            picked = jnp.where(z == k, jnp.int32(signed(values[k])), picked)
    return picked


def nibble(word, k):
    return (word >> (4 * k)) & 15


def quarter(word):
    first = (word & 15) // SPAN * SPAN
    return range(first, first + SPAN)


def targets(z):
    found = []
    for word in TREE[z]:
        for k in range(1, 8):
            d = (word >> (4 * k)) & 15
            if d != z and d not in found:
                found.append(d)
    return found


SENDS = [sum((word >> (4 * k)) & 15 != z for word in TREE[z] for k in range(1, 8)) for z in range(16)]
TARGETS = [len(targets(z)) for z in range(16)]
LAST = [
    sum(1 << k for k in range(16) if all(TREE[z][i] & 15 != q for i in range(k + 1, 16) for q in quarter(TREE[z][k])))
    for z in range(16)
]
GROUPS = tuple(q // SPAN for q in (0, 2, 4, 6, 14, 12, 10, 8)) if SPAN == 2 else (0, 1, 3, 2)
SOURCES = [sum(1 << z for z in range(16) if d in targets(z)) for d in range(16)]


def labels(position, base, occ, vir):
    first = base // NVIR
    orbital = jnp.full_like(position, first)
    for k in (1, 2):
        orbital += (position >= (first + k) * NVIR).astype(jnp.int32)
    virtual = position - orbital * NVIR
    occ_part = jnp.zeros_like(position)
    vir_part = jnp.zeros_like(position)
    occ_bound = jnp.int32(0)
    vir_bound = jnp.int32(0)
    for k in range(7):
        occ_bound += occ[k]
        vir_bound += vir[k]
        occ_part += (orbital >= occ_bound).astype(jnp.int32)
        vir_part += (virtual >= vir_bound).astype(jnp.int32)
    return occ_part ^ vir_part


def split(x):
    high = x.astype(BF16)
    return high, (x - high.astype(F32)).astype(BF16)


def product(left, right):
    dims = (((0,), (0,)), ((), ()))
    lh, ll = split(left)
    rh, rl = split(right)
    dot = lambda a, b: lax.dot_general(a, b, dims, preferred_element_type=F32)
    return dot(lh, rh) + (dot(lh, rl) + dot(ll, rh))


def kernel(
    a_hbm, b_hbm, occ_hbm, vir_hbm, o_ref,
    w, br, bc, ac, row_lab, occ, vir,
    local, w_in, br_in, bc_in, ac_in, cross_in, ap_in, share_in, ready,
    tree_out, cross_out, br_out, bc_out, ac_out, pair_out, ap_out, share_out,
):
    row = lax.axis_index("row")
    col = lax.axis_index("col")
    z = col % 16
    yhi = col // 16
    ylo = row // 8
    core = row % 2
    x = row // 2 % 4

    own = [
        pltpu.make_async_copy(a_hbm.at[:, pl.ds(256 * h, 256)], w.at[col, h], local.at[0])
        for h in (0, 1)
    ] + [
        pltpu.make_async_copy(b_hbm.at[pl.ds(8 * h, 8)], w.at[col, 2 + h], local.at[0])
        for h in (0, 1)
    ]
    small = [
        pltpu.make_async_copy(occ_hbm, occ, local.at[2]),
        pltpu.make_async_copy(vir_hbm, vir, local.at[3]),
        pltpu.make_async_copy(b_hbm.at[pl.ds(0, 8)], bc.at[row, 0], local.at[1]),
        pltpu.make_async_copy(b_hbm.at[pl.ds(8, 8)], bc.at[row, 1], local.at[1]),
    ]
    barrier = pltpu.get_barrier_semaphore()
    sources = by_z(z, SOURCES)

    def greet_z(d, carry):
        @pl.when(((sources >> d) & 1) == 1)
        def _():
            pl.semaphore_signal(
                barrier, inc=1, device_id={"row": row, "col": yhi * 16 + d}, device_id_type=MESH
            )
        return carry

    other = {"row": row + 1 - 2 * core, "col": col}
    peers = [other]
    peers += [{"row": ylo * 8 + (x + k) % 4 * 2 + core, "col": col} for k in (1, 2, 3)]
    peers += [
        {"row": (ylo + k % 2) % 2 * 8 + x * 2 + core, "col": (yhi + k // 2) % 2 * 16 + z} for k in (1, 2, 3)
    ]
    late = z >= 8

    @pl.when(late)
    def _():
        for peer in peers:
            pl.semaphore_signal(barrier, inc=1, device_id=peer, device_id_type=MESH)

    @pl.when(jnp.logical_not(late))
    def _():
        def greet_plane(t, carry):
            r, y = t % 16, t // 16

            @pl.when(jnp.logical_or(r != row, y != yhi))
            def _():
                pl.semaphore_signal(
                    barrier, inc=1, device_id={"row": r, "col": y * 16 + z}, device_id_type=MESH
                )
            return carry

        lax.fori_loop(0, 32, greet_plane, 0)

    lax.fori_loop(0, 16, greet_z, 0)
    for copy in own + small:
        copy.start()

    share = ylo * 8 + (x - z // 4 + 6) % 4 * 2 + core
    early = jnp.logical_not(late)
    shares = jnp.logical_and(early, share % 8 >= 4)
    direct = jnp.logical_and(late, x < 2)

    @pl.when(shares)
    def _():
        for e in (0, 1):
            pl.semaphore_signal(
                barrier, inc=1, device_id={"row": col // 2, "col": 2 * share + e}, device_id_type=MESH
            )

    def label_rows():
        small[0].wait()
        small[1].wait()
        pltpu.make_async_copy(bc.at[0], bc.at[0], local.at[1]).wait()
        row_pos = row * 512 + lax.broadcasted_iota(jnp.int32, (512, 128), 0)
        row_lab[...] = labels(row_pos, row * 512, occ, vir)

    @pl.when(early)
    def _():
        label_rows()

    pl.semaphore_wait(
        barrier, jnp.where(late, 7, 31) + by_z(z, TARGETS) + 2 * direct.astype(jnp.int32)
    )

    @pl.when(late)
    def _():
        for peer in peers:
            pl.semaphore_signal(ready.at[0], inc=1, device_id=peer, device_id_type=MESH)

    pltpu.make_async_copy(w.at[0], w.at[0], local.at[0]).wait()

    def send_tree(s, d):
        c = yhi * 16 + s
        pltpu.make_async_remote_copy(
            src_ref=w.at[c], dst_ref=w.at[c], send_sem=tree_out, recv_sem=w_in.at[s],
            device_id={"row": row, "col": yhi * 16 + d}, device_id_type=MESH,
        ).start()

    def cross(s):
        c = yhi * 16 + s
        return pltpu.make_async_remote_copy(
            src_ref=w.at[c, pl.ds(0, 2)], dst_ref=w.at[c, pl.ds(0, 2)], send_sem=cross_out,
            recv_sem=cross_in, device_id={"row": row, "col": (1 - yhi) * 16 + z}, device_id_type=MESH,
        )

    def to_rows(s, y):
        r = yhi * 8 + s // 2
        source = w.at[yhi * 16 + s, pl.ds(2, 2)]
        me = jnp.logical_and(r == row, y == yhi)

        @pl.when(me)
        def _():
            pltpu.make_async_copy(source, br.at[row, s % 2], br_in).start()

        @pl.when(jnp.logical_not(me))
        def _():
            pltpu.make_async_remote_copy(
                src_ref=source, dst_ref=br.at[row, s % 2], send_sem=br_out, recv_sem=br_in,
                device_id={"row": r, "col": y * 16 + z}, device_id_type=MESH,
            ).start()

    owner = row % 8 == z // 2
    half = z % 2

    def to_plane(g):
        c = yhi * 16 + SPAN * g
        t = yhi * (16 // SPAN) + g
        source = w.at[pl.ds(c, SPAN), half]

        def one(chip, carry):
            r = 2 * chip + core
            me = jnp.logical_and(r == row, ylo == yhi)

            @pl.when(me)
            def _():
                pltpu.make_async_copy(source, ac.at[pl.ds(c, SPAN)], ac_in.at[t]).start()

            @pl.when(jnp.logical_not(me))
            def _():
                pltpu.make_async_remote_copy(
                    src_ref=source, dst_ref=ac.at[pl.ds(c, SPAN)], send_sem=ac_out,
                    recv_sem=ac_in.at[t],
                    device_id={"row": r, "col": ylo * 16 + z}, device_id_type=MESH,
                ).start()
            return carry

        lax.fori_loop(0, 8, one, 0)

    def direct_to(h):
        r = yhi * 8 + (x + z // 4 + 2) % 4 * 2 + z // 2 % 2
        return pltpu.make_async_remote_copy(
            src_ref=w.at[col, h], dst_ref=ac.at[col], send_sem=ap_out, recv_sem=ap_in,
            device_id={"row": r, "col": 2 * row + h}, device_id_type=MESH,
        )

    share_piece = ac.at[pl.ds(2 * share, 2)]

    @pl.when(direct)
    def _():
        direct_to(0).start()
        direct_to(1).start()

    last = by_z(z, LAST)
    for k in range(16):
        word = by_z(z, [TREE[v][k] for v in range(16)])
        s = nibble(word, 0)
        if k:
            pltpu.make_async_copy(w.at[s], w.at[s], w_in.at[s]).wait()

        def forward(i, carry):
            d = (word >> (4 * i)) & 15
            there = d != z

            @pl.when(there)
            def _():
                send_tree(s, d)
            return carry

        lax.fori_loop(1, 8, forward, 0)
        if k == 0:
            @pl.when(late)
            def _():
                pl.semaphore_wait(ready.at[0], 7)
                pl.semaphore_signal(ready.at[1], inc=1, device_id=other, device_id_type=MESH)
                pl.semaphore_wait(ready.at[1], 1)
        @pl.when(
            jnp.logical_and(jnp.logical_and(owner, ((last >> k) & 1) == 1), jnp.logical_or(late, s < 8))
        )
        def _():
            to_plane(s // SPAN)

        cross(s).start()
        to_rows(s, 0)
        to_rows(s, 1)


        if k == 0:
            def give(r, carry):
                @pl.when(r != row)
                def _():
                    pltpu.make_async_remote_copy(
                        src_ref=w.at[col, pl.ds(2, 2)], dst_ref=bc.at[row], send_sem=bc_out,
                        recv_sem=bc_in, device_id={"row": r, "col": col}, device_id_type=MESH,
                    ).start()
                return carry

            lax.fori_loop(0, 16, give, 0)

            @pl.when(late)
            def _():
                label_rows()

        if k == SHARE_AFTER:
            @pl.when(shares)
            def _():
                pltpu.make_async_copy(share_piece, share_piece, ap_in).wait()

                def give_share(r, carry):
                    @pl.when(r != row)
                    def _():
                        pltpu.make_async_remote_copy(
                            src_ref=share_piece, dst_ref=share_piece, send_sem=share_out,
                            recv_sem=share_in, device_id={"row": r, "col": col}, device_id_type=MESH,
                        ).start()
                    return carry

                lax.fori_loop(0, 16, give_share, 0)

    first = core == (z // 2) % 2

    def group(t):
        return ac.at[pl.ds(SPAN * t, SPAN)]

    for g in GROUPS:
        @pl.when(jnp.logical_and(first, late) if g * SPAN >= 8 else first)
        def _():
            for y in (0, 1):
                t = 16 // SPAN * y + g
                pltpu.make_async_copy(group(t), group(t), ac_in.at[t]).wait()
                pltpu.make_async_remote_copy(
                    src_ref=group(t), dst_ref=group(t), send_sem=pair_out,
                    recv_sem=ac_in.at[t], device_id={"row": 2 * (row // 2) + 1 - core, "col": col},
                    device_id_type=MESH,
                ).start()

    pltpu.make_async_copy(bc.at[pl.ds(0, 15)], bc.at[pl.ds(0, 15)], bc_in).wait()
    pltpu.make_async_copy(ac, ac, cross_in).wait()
    b_here = bc[...].reshape(256, 256)
    for m in (0, 1):
        o_ref[256 * m : 256 * (m + 1)] = product(w[:, m].reshape(256, 256), b_here)

    pltpu.make_async_copy(br, br, br_in).wait()

    for t in range(32 // SPAN):
        here = jnp.logical_not(first)

        @pl.when(jnp.logical_and(here, late) if t * SPAN % 16 >= 8 else here)
        def _():
            pltpu.make_async_copy(group(t), group(t), ac_in.at[t]).wait()

    @pl.when(shares)
    def _():
        pltpu.make_async_copy(ac.at[pl.ds(0, 14)], ac.at[pl.ds(0, 14)], share_in).wait()

    @pl.when(jnp.logical_and(early, jnp.logical_not(shares)))
    def _():
        pltpu.make_async_copy(ac.at[pl.ds(0, 16)], ac.at[pl.ds(0, 16)], share_in).wait()

    col_lab = labels(
        col * 256 + lax.broadcasted_iota(jnp.int32, (8, 256), 1), col * 256, occ, vir
    )[:1]
    a_here = ac[...].reshape(256, 256)
    for m in (0, 1):
        rows = slice(256 * m, 256 * (m + 1))
        total = o_ref[rows] + product(br[:, m].reshape(256, 256), a_here)
        lab = row_lab[rows]
        for h in (0, 1):
            lanes = slice(128 * h, 128 * (h + 1))
            o_ref[rows, lanes] = jnp.where(lab == col_lab[:, lanes], total[:, lanes], 0.0)

    count = by_z(z, SENDS)
    for n in sorted(set(SENDS)):
        @pl.when(count == n)
        def _():
            pltpu.make_async_copy(w.at[pl.ds(0, n)], w.at[pl.ds(0, n)], tree_out).wait()

    pltpu.make_async_copy(ac, ac, cross_out).wait()
    pltpu.make_async_copy(bc.at[pl.ds(0, 15)], bc.at[pl.ds(0, 15)], bc_out).wait()

    @pl.when(ylo == yhi)
    def _():
        pltpu.make_async_copy(br.at[pl.ds(0, 15)], br.at[pl.ds(0, 15)], br_out).wait()

    @pl.when(ylo != yhi)
    def _():
        pltpu.make_async_copy(br, br, br_out).wait()

    for when, chips in ((ylo == yhi, 7), (ylo != yhi, 8)):
        for plane, pieces in ((early, 2 * chips), (late, 4 * chips)):
            @pl.when(jnp.logical_and(owner, jnp.logical_and(when, plane)))
            def _():
                pltpu.make_async_copy(w.at[pl.ds(0, pieces)], w.at[pl.ds(0, pieces)], ac_out).wait()

    for plane, pieces in ((early, 16), (late, 32)):
        @pl.when(jnp.logical_and(first, plane))
        def _():
            pltpu.make_async_copy(ac.at[pl.ds(0, pieces)], ac.at[pl.ds(0, pieces)], pair_out).wait()

    @pl.when(direct)
    def _():
        pltpu.make_async_copy(ac.at[pl.ds(0, 2)], ac.at[pl.ds(0, 2)], ap_out).wait()

    @pl.when(shares)
    def _():
        pltpu.make_async_copy(ac.at[pl.ds(0, 30)], ac.at[pl.ds(0, 30)], share_out).wait()


def per_device(amplitudes, integrals, occ_counts, vir_counts):
    arrays = (amplitudes.T, integrals, occ_counts, vir_counts)
    hbm = pl.BlockSpec(memory_space=pltpu.HBM)
    dma = pltpu.SemaphoreType.DMA
    return pl.pallas_call(
        kernel,
        out_shape=jax.ShapeDtypeStruct((512, 256), F32),
        in_specs=[hbm, hbm, hbm, hbm],
        out_specs=pl.BlockSpec(memory_space=pltpu.VMEM),
        scratch_shapes=[
            pltpu.VMEM((32, 4, 8, 256), F32),
            pltpu.VMEM((16, 2, 2, 8, 256), F32),
            pltpu.VMEM((16, 2, 8, 256), F32),
            pltpu.VMEM((32, 8, 256), F32),
            pltpu.VMEM((512, 128), jnp.int32),
            pltpu.SMEM((8,), jnp.int32),
            pltpu.SMEM((8,), jnp.int32),
            dma((4,)), dma((16,)), dma, dma, dma((32 // SPAN,)), dma,
            dma, dma, pltpu.SemaphoreType.REGULAR((2,)),
            dma, dma, dma, dma, dma, dma, dma, dma,
        ],
        compiler_params=pltpu.CompilerParams(
            collective_id=0, has_side_effects=True, vmem_limit_bytes=32 * 2**20
        ),
    )(*[pltpu.with_memory_space_constraint(v, pltpu.HBM) for v in arrays])


def solution(mesh):
    placed = (P("row", "col"), P("row", "col"), P(), P())
    return jax.shard_map(
        per_device, mesh=mesh, in_specs=placed, out_specs=P("row", "col"), check_vma=False
    )
```

```python
import jax
import jax.numpy as jnp
from jax import lax
from jax.experimental import pallas as pl
from jax.experimental.pallas import tpu as pltpu
from jax.sharding import PartitionSpec as P

NVIR = 400
SPAN = 2
SHARE_AFTER = 10
MESH = pl.DeviceIdType.MESH
F32 = jnp.float32
BF16 = jnp.bfloat16

TREE = (
    (0x002fd1e0, 0x000000f4, 0x000000c1, 0x0000001f, 0x000000e3, 0x0000013e, 0x000000f5, 0x00000df2,
     0x00000e1b, 0x00000d19, 0x0000003c, 0x00000fed, 0x00000007, 0x0000000a, 0x000000d8, 0x00000ef6),
    (0x11142f01, 0x11111032, 0x11111113, 0x11111130, 0x11111114, 0x11111115, 0x1111120d, 0x11111107,
     0x1111111f, 0x1111203a, 0x1111112e, 0x1111123b, 0x111111fc, 0x11111119, 0x111111f8, 0x11111116),
    (0x22226412, 0x22222224, 0x22222361, 0x22222223, 0x22222240, 0x22222347, 0x2222222f, 0x22222225,
     0x22222208, 0x2222243d, 0x22222229, 0x2222222a, 0x22222246, 0x2222222e, 0x2222222c, 0x2222222b),
    (0x33264013, 0x33333614, 0x33333425, 0x3333364f, 0x33333351, 0x33333332, 0x33351206, 0x33333350,
     0x33333338, 0x3333345e, 0x33333339, 0x33333337, 0x3333333a, 0x3333333d, 0x3333333c, 0x3333333b),
    (0x44430254, 0x44444453, 0x44444452, 0x44444441, 0x44443529, 0x44444445, 0x4444445f, 0x44444440,
     0x4444444a, 0x44444447, 0x4444444b, 0x4444444c, 0x4444444e, 0x4444444d, 0x44444448, 0x44444446),
    (0x55613705, 0x55555574, 0x55555553, 0x55555572, 0x5555547b, 0x5555524c, 0x55555769, 0x55555571,
     0x55555558, 0x5555555f, 0x55555556, 0x55555760, 0x5555555d, 0x5555555e, 0x55555557, 0x5555555a),
    (0x66666736, 0x66666665, 0x66667d93, 0x66666692, 0x66666664, 0x66666661, 0x6666666d, 0x66666648,
     0x6666667f, 0x66666657, 0x6666665a, 0x666666e9, 0x6666666c, 0x6666666b, 0x66666660, 0x6666666e),
    (0x77728917, 0x77777985, 0x77777784, 0x77777568, 0x77777786, 0x77777783, 0x77777772, 0x7777776c,
     0x7777768b, 0x7777779e, 0x7777777d, 0x7777778f, 0x77777779, 0x77777771, 0x7777777a, 0x77777770),
    (0x8897c328, 0x8888884a, 0x88888887, 0x888888b5, 0x88888894, 0x88888889, 0x8889bcd6, 0x88888883,
     0x8888888c, 0x8888888d, 0x88888882, 0x8888888b, 0x8888888f, 0x88888880, 0x88888881, 0x8888888e),
    (0x999c0a49, 0x99996ca7, 0x99999b6a, 0x999999ab, 0x99999998, 0x999999c5, 0x999999a3, 0x9999997d,
     0x99999994, 0x99999982, 0x9999999c, 0x999999cf, 0x999999a6, 0x9999998e, 0x99999990, 0x99999991),
    (0xaaac198a, 0xaaaaaa89, 0xaaaaaaa7, 0xaaaaa98c, 0xaaaaaa8d, 0xaaaaaacb, 0xaaaaaa6e, 0xaaaaabc3,
     0xaaaaa890, 0xaaaaaaa8, 0xaaaaa891, 0xaaaaaac4, 0xaaaaaaa5, 0xaaaaaaaf, 0xaaaaaaa6, 0xaaaaaaa2),
    (0xbbbb509b, 0xbbbbba7c, 0xbbbb5a9d, 0xbbbbbb7e, 0xbbbbbd9f, 0xbbbbbb7a, 0xbbbbbac0, 0xbbbbbae8,
     0xbbbbbbd5, 0xbbbbbbb7, 0xbbbbbbb1, 0xbbbbbbb4, 0xbbbbbbb3, 0xbbbbbba2, 0xbbbbbbb6, 0xbbbbbbb9),
    (0xcccc5bdc, 0xccccceda, 0xcccccccd, 0xccccccf9, 0xcccccb18, 0xcccccafe, 0xccccdeb7, 0xcccccda1,
     0xcccccae5, 0xccccccc0, 0xcccccccb, 0xccccccc2, 0xccccccc6, 0xccccccc3, 0xcccccccf, 0xccccccc4),
    (0xdddc16bd, 0xddddd10c, 0xddddddce, 0xddddddb0, 0xddddddfa, 0xdddddba4, 0xddddebc2, 0xddddddaf,
     0xddddddb9, 0xddddddf7, 0xddddddd1, 0xddddddf3, 0xdddddddb, 0xddddddd8, 0xddddddd5, 0xddddddd6),
    (0xeeeedb0e, 0xeeeeeebf, 0xeeeeeee0, 0xeeeeeee3, 0xeeeeeeb1, 0xeeeeeeea, 0xeeeeeee4, 0xeeeeedfb,
     0xeeeeeee7, 0xeeeeeeed, 0xeeeeeee2, 0xeeeeeee8, 0xeeeeeee5, 0xeeeeeee6, 0xeeeeeeec, 0xeeeeeee9),
    (0xfff20e3f, 0xfffffff0, 0xffffffe1, 0xfffffed4, 0xfffffff5, 0xfffffff2, 0xfffffff9, 0xfffffffa,
     0xfffffffe, 0xfffffffd, 0xffffffec, 0xfffffffb, 0xfffffff6, 0xfffffff8, 0xfffffff7, 0xfffffff3),
)

def signed(word):
    return word - (1 << 32) if word >= 1 << 31 else word


def by_z(z, values):
    picked = jnp.int32(signed(values[0]))
    for k in range(1, 16):
        if values[k] != values[0]:
            picked = jnp.where(z == k, jnp.int32(signed(values[k])), picked)
    return picked


def nibble(word, k):
    return (word >> (4 * k)) & 15


def quarter(word):
    first = (word & 15) // SPAN * SPAN
    return range(first, first + SPAN)


def targets(z):
    found = []
    for word in TREE[z]:
        for k in range(1, 8):
            d = (word >> (4 * k)) & 15
            if d != z and d not in found:
                found.append(d)
    return found


SENDS = [sum((word >> (4 * k)) & 15 != z for word in TREE[z] for k in range(1, 8)) for z in range(16)]
TARGETS = [len(targets(z)) for z in range(16)]
LAST = [
    sum(1 << k for k in range(16) if all(TREE[z][i] & 15 != q for i in range(k + 1, 16) for q in quarter(TREE[z][k])))
    for z in range(16)
]
GROUPS = tuple(q // SPAN for q in (0, 2, 4, 6, 14, 12, 10, 8)) if SPAN == 2 else (0, 1, 3, 2)
SOURCES = [sum(1 << z for z in range(16) if d in targets(z)) for d in range(16)]


def labels(position, base, occ, vir):
    first = base // NVIR
    orbital = jnp.full_like(position, first)
    for k in (1, 2):
        orbital += (position >= (first + k) * NVIR).astype(jnp.int32)
    virtual = position - orbital * NVIR
    occ_part = jnp.zeros_like(position)
    vir_part = jnp.zeros_like(position)
    occ_bound = jnp.int32(0)
    vir_bound = jnp.int32(0)
    for k in range(7):
        occ_bound += occ[k]
        vir_bound += vir[k]
        occ_part += (orbital >= occ_bound).astype(jnp.int32)
        vir_part += (virtual >= vir_bound).astype(jnp.int32)
    return occ_part ^ vir_part


def split(x):
    high = x.astype(BF16)
    return high, (x - high.astype(F32)).astype(BF16)


def product(left, right):
    dims = (((0,), (0,)), ((), ()))
    lh, ll = split(left)
    rh, rl = split(right)
    dot = lambda a, b: lax.dot_general(a, b, dims, preferred_element_type=F32)
    return dot(lh, rh) + (dot(lh, rl) + dot(ll, rh))


def kernel(
    a_hbm, b_hbm, occ_hbm, vir_hbm, o_ref,
    w, br, bc, ac, row_lab, occ, vir,
    local, w_in, br_in, bc_in, ac_in, cross_in, ap_in, share_in, ready,
    tree_out, cross_out, br_out, bc_out, ac_out, pair_out, ap_out, share_out,
):
    row = lax.axis_index("row")
    col = lax.axis_index("col")
    z = col % 16
    yhi = col // 16
    ylo = row // 8
    core = row % 2
    x = row // 2 % 4

    own = [
        pltpu.make_async_copy(a_hbm.at[:, pl.ds(256 * h, 256)], w.at[col, h], local.at[0])
        for h in (0, 1)
    ] + [
        pltpu.make_async_copy(b_hbm.at[pl.ds(8 * h, 8)], w.at[col, 2 + h], local.at[0])
        for h in (0, 1)
    ]
    small = [
        pltpu.make_async_copy(occ_hbm, occ, local.at[2]),
        pltpu.make_async_copy(vir_hbm, vir, local.at[3]),
        pltpu.make_async_copy(b_hbm.at[pl.ds(0, 8)], bc.at[row, 0], local.at[1]),
        pltpu.make_async_copy(b_hbm.at[pl.ds(8, 8)], bc.at[row, 1], local.at[1]),
    ]
    barrier = pltpu.get_barrier_semaphore()
    sources = by_z(z, SOURCES)

    def greet_z(d, carry):
        @pl.when(((sources >> d) & 1) == 1)
        def _():
            pl.semaphore_signal(
                barrier, inc=1, device_id={"row": row, "col": yhi * 16 + d}, device_id_type=MESH
            )
        return carry

    other = {"row": row + 1 - 2 * core, "col": col}
    peers = [other]
    peers += [{"row": ylo * 8 + (x + k) % 4 * 2 + core, "col": col} for k in (1, 2, 3)]
    peers += [
        {"row": (ylo + k % 2) % 2 * 8 + x * 2 + core, "col": (yhi + k // 2) % 2 * 16 + z} for k in (1, 2, 3)
    ]
    late = z >= 8

    @pl.when(late)
    def _():
        for peer in peers:
            pl.semaphore_signal(barrier, inc=1, device_id=peer, device_id_type=MESH)

    @pl.when(jnp.logical_not(late))
    def _():
        def greet_plane(t, carry):
            r, y = t % 16, t // 16

            @pl.when(jnp.logical_or(r != row, y != yhi))
            def _():
                pl.semaphore_signal(
                    barrier, inc=1, device_id={"row": r, "col": y * 16 + z}, device_id_type=MESH
                )
            return carry

        lax.fori_loop(0, 32, greet_plane, 0)

    lax.fori_loop(0, 16, greet_z, 0)
    for copy in own + small:
        copy.start()

    share = ylo * 8 + (x - z // 4 + 6) % 4 * 2 + core
    early = jnp.logical_not(late)
    shares = jnp.logical_and(early, share % 8 >= 4)
    direct = jnp.logical_and(late, x < 2)

    @pl.when(shares)
    def _():
        for e in (0, 1):
            pl.semaphore_signal(
                barrier, inc=1, device_id={"row": col // 2, "col": 2 * share + e}, device_id_type=MESH
            )

    def label_rows():
        small[0].wait()
        small[1].wait()
        pltpu.make_async_copy(bc.at[0], bc.at[0], local.at[1]).wait()
        row_pos = row * 512 + lax.broadcasted_iota(jnp.int32, (512, 128), 0)
        row_lab[...] = labels(row_pos, row * 512, occ, vir)

    @pl.when(early)
    def _():
        label_rows()

    pl.semaphore_wait(
        barrier, jnp.where(late, 7, 31) + by_z(z, TARGETS) + 2 * direct.astype(jnp.int32)
    )

    @pl.when(late)
    def _():
        for peer in peers:
            pl.semaphore_signal(ready.at[0], inc=1, device_id=peer, device_id_type=MESH)

    pltpu.make_async_copy(w.at[0], w.at[0], local.at[0]).wait()

    def send_tree(s, d):
        c = yhi * 16 + s
        pltpu.make_async_remote_copy(
            src_ref=w.at[c], dst_ref=w.at[c], send_sem=tree_out, recv_sem=w_in.at[s],
            device_id={"row": row, "col": yhi * 16 + d}, device_id_type=MESH,
        ).start()

    def cross(s):
        c = yhi * 16 + s
        return pltpu.make_async_remote_copy(
            src_ref=w.at[c, pl.ds(0, 2)], dst_ref=w.at[c, pl.ds(0, 2)], send_sem=cross_out,
            recv_sem=cross_in, device_id={"row": row, "col": (1 - yhi) * 16 + z}, device_id_type=MESH,
        )

    def to_rows(s, y):
        r = yhi * 8 + s // 2
        source = w.at[yhi * 16 + s, pl.ds(2, 2)]
        me = jnp.logical_and(r == row, y == yhi)

        @pl.when(me)
        def _():
            pltpu.make_async_copy(source, br.at[row, s % 2], br_in).start()

        @pl.when(jnp.logical_not(me))
        def _():
            pltpu.make_async_remote_copy(
                src_ref=source, dst_ref=br.at[row, s % 2], send_sem=br_out, recv_sem=br_in,
                device_id={"row": r, "col": y * 16 + z}, device_id_type=MESH,
            ).start()

    owner = row % 8 == z // 2
    half = z % 2

    def to_plane(g):
        c = yhi * 16 + SPAN * g
        t = yhi * (16 // SPAN) + g
        source = w.at[pl.ds(c, SPAN), half]

        def one(chip, carry):
            r = 2 * chip + core
            me = jnp.logical_and(r == row, ylo == yhi)

            @pl.when(me)
            def _():
                pltpu.make_async_copy(source, ac.at[pl.ds(c, SPAN)], ac_in.at[t]).start()

            @pl.when(jnp.logical_not(me))
            def _():
                pltpu.make_async_remote_copy(
                    src_ref=source, dst_ref=ac.at[pl.ds(c, SPAN)], send_sem=ac_out,
                    recv_sem=ac_in.at[t],
                    device_id={"row": r, "col": ylo * 16 + z}, device_id_type=MESH,
                ).start()
            return carry

        lax.fori_loop(0, 8, one, 0)

    def direct_to(h):
        r = yhi * 8 + (x + z // 4 + 2) % 4 * 2 + z // 2 % 2
        return pltpu.make_async_remote_copy(
            src_ref=w.at[col, h], dst_ref=ac.at[col], send_sem=ap_out, recv_sem=ap_in,
            device_id={"row": r, "col": 2 * row + h}, device_id_type=MESH,
        )

    share_piece = ac.at[pl.ds(2 * share, 2)]

    @pl.when(direct)
    def _():
        direct_to(0).start()
        direct_to(1).start()

    last = by_z(z, LAST)
    for k in range(16):
        word = by_z(z, [TREE[v][k] for v in range(16)])
        s = nibble(word, 0)
        if k:
            pltpu.make_async_copy(w.at[s], w.at[s], w_in.at[s]).wait()

        def forward(i, carry):
            d = (word >> (4 * i)) & 15
            there = d != z

            @pl.when(there)
            def _():
                send_tree(s, d)
            return carry

        lax.fori_loop(1, 8, forward, 0)
        if k == 0:
            @pl.when(late)
            def _():
                pl.semaphore_wait(ready.at[0], 7)
                pl.semaphore_signal(ready.at[1], inc=1, device_id=other, device_id_type=MESH)
                pl.semaphore_wait(ready.at[1], 1)
        @pl.when(
            jnp.logical_and(jnp.logical_and(owner, ((last >> k) & 1) == 1), jnp.logical_or(late, s < 8))
        )
        def _():
            to_plane(s // SPAN)

        cross(s).start()
        to_rows(s, 0)
        to_rows(s, 1)


        if k == 0:
            def give(r, carry):
                @pl.when(r != row)
                def _():
                    pltpu.make_async_remote_copy(
                        src_ref=w.at[col, pl.ds(2, 2)], dst_ref=bc.at[row], send_sem=bc_out,
                        recv_sem=bc_in, device_id={"row": r, "col": col}, device_id_type=MESH,
                    ).start()
                return carry

            lax.fori_loop(0, 16, give, 0)

            @pl.when(late)
            def _():
                label_rows()

        if k == SHARE_AFTER:
            @pl.when(shares)
            def _():
                pltpu.make_async_copy(share_piece, share_piece, ap_in).wait()

                def give_share(r, carry):
                    @pl.when(r != row)
                    def _():
                        pltpu.make_async_remote_copy(
                            src_ref=share_piece, dst_ref=share_piece, send_sem=share_out,
                            recv_sem=share_in, device_id={"row": r, "col": col}, device_id_type=MESH,
                        ).start()
                    return carry

                lax.fori_loop(0, 16, give_share, 0)

    first = core == (z // 2) % 2

    def group(t):
        return ac.at[pl.ds(SPAN * t, SPAN)]

    for g in GROUPS:
        @pl.when(jnp.logical_and(first, late) if g * SPAN >= 8 else first)
        def _():
            for y in (0, 1):
                t = 16 // SPAN * y + g
                pltpu.make_async_copy(group(t), group(t), ac_in.at[t]).wait()
                pltpu.make_async_remote_copy(
                    src_ref=group(t), dst_ref=group(t), send_sem=pair_out,
                    recv_sem=ac_in.at[t], device_id={"row": 2 * (row // 2) + 1 - core, "col": col},
                    device_id_type=MESH,
                ).start()

    col_lab = labels(
        col * 256 + lax.broadcasted_iota(jnp.int32, (8, 256), 1), col * 256, occ, vir
    )[:1]

    pltpu.make_async_copy(bc.at[pl.ds(0, 15)], bc.at[pl.ds(0, 15)], bc_in).wait()
    pltpu.make_async_copy(ac, ac, cross_in).wait()
    b_here = bc[...].reshape(256, 256)
    for m in (0, 1):
        o_ref[256 * m : 256 * (m + 1)] = product(w[:, m].reshape(256, 256), b_here)

    pltpu.make_async_copy(br, br, br_in).wait()

    for t in range(32 // SPAN):
        here = jnp.logical_not(first)

        @pl.when(jnp.logical_and(here, late) if t * SPAN % 16 >= 8 else here)
        def _():
            pltpu.make_async_copy(group(t), group(t), ac_in.at[t]).wait()

    @pl.when(shares)
    def _():
        pltpu.make_async_copy(ac.at[pl.ds(0, 14)], ac.at[pl.ds(0, 14)], share_in).wait()

    @pl.when(jnp.logical_and(early, jnp.logical_not(shares)))
    def _():
        pltpu.make_async_copy(ac.at[pl.ds(0, 16)], ac.at[pl.ds(0, 16)], share_in).wait()

    a_here = ac[...].reshape(256, 256)
    for m in (0, 1):
        rows = slice(256 * m, 256 * (m + 1))
        total = o_ref[rows] + product(br[:, m].reshape(256, 256), a_here)
        lab = row_lab[rows]
        for h in (0, 1):
            lanes = slice(128 * h, 128 * (h + 1))
            o_ref[rows, lanes] = jnp.where(lab == col_lab[:, lanes], total[:, lanes], 0.0)

    count = by_z(z, SENDS)
    for n in sorted(set(SENDS)):
        @pl.when(count == n)
        def _():
            pltpu.make_async_copy(w.at[pl.ds(0, n)], w.at[pl.ds(0, n)], tree_out).wait()

    pltpu.make_async_copy(ac, ac, cross_out).wait()
    pltpu.make_async_copy(bc.at[pl.ds(0, 15)], bc.at[pl.ds(0, 15)], bc_out).wait()

    @pl.when(ylo == yhi)
    def _():
        pltpu.make_async_copy(br.at[pl.ds(0, 15)], br.at[pl.ds(0, 15)], br_out).wait()

    @pl.when(ylo != yhi)
    def _():
        pltpu.make_async_copy(br, br, br_out).wait()

    for when, chips in ((ylo == yhi, 7), (ylo != yhi, 8)):
        for plane, pieces in ((early, 2 * chips), (late, 4 * chips)):
            @pl.when(jnp.logical_and(owner, jnp.logical_and(when, plane)))
            def _():
                pltpu.make_async_copy(w.at[pl.ds(0, pieces)], w.at[pl.ds(0, pieces)], ac_out).wait()

    for plane, pieces in ((early, 16), (late, 32)):
        @pl.when(jnp.logical_and(first, plane))
        def _():
            pltpu.make_async_copy(ac.at[pl.ds(0, pieces)], ac.at[pl.ds(0, pieces)], pair_out).wait()

    @pl.when(direct)
    def _():
        pltpu.make_async_copy(ac.at[pl.ds(0, 2)], ac.at[pl.ds(0, 2)], ap_out).wait()

    @pl.when(shares)
    def _():
        pltpu.make_async_copy(ac.at[pl.ds(0, 30)], ac.at[pl.ds(0, 30)], share_out).wait()


def per_device(amplitudes, integrals, occ_counts, vir_counts):
    arrays = (amplitudes.T, integrals, occ_counts, vir_counts)
    hbm = pl.BlockSpec(memory_space=pltpu.HBM)
    dma = pltpu.SemaphoreType.DMA
    return pl.pallas_call(
        kernel,
        out_shape=jax.ShapeDtypeStruct((512, 256), F32),
        in_specs=[hbm, hbm, hbm, hbm],
        out_specs=pl.BlockSpec(memory_space=pltpu.VMEM),
        scratch_shapes=[
            pltpu.VMEM((32, 4, 8, 256), F32),
            pltpu.VMEM((16, 2, 2, 8, 256), F32),
            pltpu.VMEM((16, 2, 8, 256), F32),
            pltpu.VMEM((32, 8, 256), F32),
            pltpu.VMEM((512, 128), jnp.int32),
            pltpu.SMEM((8,), jnp.int32),
            pltpu.SMEM((8,), jnp.int32),
            dma((4,)), dma((16,)), dma, dma, dma((32 // SPAN,)), dma,
            dma, dma, pltpu.SemaphoreType.REGULAR((2,)),
            dma, dma, dma, dma, dma, dma, dma, dma,
        ],
        compiler_params=pltpu.CompilerParams(
            collective_id=0, has_side_effects=True, vmem_limit_bytes=32 * 2**20
        ),
    )(*[pltpu.with_memory_space_constraint(v, pltpu.HBM) for v in arrays])


def solution(mesh):
    placed = (P("row", "col"), P("row", "col"), P(), P())
    return jax.shard_map(
        per_device, mesh=mesh, in_specs=placed, out_specs=P("row", "col"), check_vma=False
    )
```

```python
import jax
import jax.numpy as jnp
from jax import lax
from jax.experimental import pallas as pl
from jax.experimental.pallas import tpu as pltpu
from jax.sharding import PartitionSpec as P

NVIR = 400
SPAN = 2
SHARE_AFTER = 10
MESH = pl.DeviceIdType.MESH
F32 = jnp.float32
BF16 = jnp.bfloat16

TREE = (
    (0x002fd1e0, 0x000000f4, 0x000000c1, 0x0000001f, 0x000000e3, 0x0000013e, 0x000000f5, 0x00000df2,
     0x00000e1b, 0x00000d19, 0x0000003c, 0x00000fed, 0x00000007, 0x0000000a, 0x000000d8, 0x00000ef6),
    (0x11142f01, 0x11111032, 0x11111113, 0x11111130, 0x11111114, 0x11111115, 0x1111120d, 0x11111107,
     0x1111111f, 0x1111203a, 0x1111112e, 0x1111123b, 0x111111fc, 0x11111119, 0x111111f8, 0x11111116),
    (0x22226412, 0x22222224, 0x22222361, 0x22222223, 0x22222240, 0x22222347, 0x2222222f, 0x22222225,
     0x22222208, 0x2222243d, 0x22222229, 0x2222222a, 0x22222246, 0x2222222e, 0x2222222c, 0x2222222b),
    (0x33264013, 0x33333614, 0x33333425, 0x3333364f, 0x33333351, 0x33333332, 0x33351206, 0x33333350,
     0x33333338, 0x3333345e, 0x33333339, 0x33333337, 0x3333333a, 0x3333333d, 0x3333333c, 0x3333333b),
    (0x44430254, 0x44444453, 0x44444452, 0x44444441, 0x44443529, 0x44444445, 0x4444445f, 0x44444440,
     0x4444444a, 0x44444447, 0x4444444b, 0x4444444c, 0x4444444e, 0x4444444d, 0x44444448, 0x44444446),
    (0x55613705, 0x55555574, 0x55555553, 0x55555572, 0x5555547b, 0x5555524c, 0x55555769, 0x55555571,
     0x55555558, 0x5555555f, 0x55555556, 0x55555760, 0x5555555d, 0x5555555e, 0x55555557, 0x5555555a),
    (0x66666736, 0x66666665, 0x66667d93, 0x66666692, 0x66666664, 0x66666661, 0x6666666d, 0x66666648,
     0x6666667f, 0x66666657, 0x6666665a, 0x666666e9, 0x6666666c, 0x6666666b, 0x66666660, 0x6666666e),
    (0x77728917, 0x77777985, 0x77777784, 0x77777568, 0x77777786, 0x77777783, 0x77777772, 0x7777776c,
     0x7777768b, 0x7777779e, 0x7777777d, 0x7777778f, 0x77777779, 0x77777771, 0x7777777a, 0x77777770),
    (0x8897c328, 0x8888884a, 0x88888887, 0x888888b5, 0x88888894, 0x88888889, 0x8889bcd6, 0x88888883,
     0x8888888c, 0x8888888d, 0x88888882, 0x8888888b, 0x8888888f, 0x88888880, 0x88888881, 0x8888888e),
    (0x999c0a49, 0x99996ca7, 0x99999b6a, 0x999999ab, 0x99999998, 0x999999c5, 0x999999a3, 0x9999997d,
     0x99999994, 0x99999982, 0x9999999c, 0x999999cf, 0x999999a6, 0x9999998e, 0x99999990, 0x99999991),
    (0xaaac198a, 0xaaaaaa89, 0xaaaaaaa7, 0xaaaaa98c, 0xaaaaaa8d, 0xaaaaaacb, 0xaaaaaa6e, 0xaaaaabc3,
     0xaaaaa890, 0xaaaaaaa8, 0xaaaaa891, 0xaaaaaac4, 0xaaaaaaa5, 0xaaaaaaaf, 0xaaaaaaa6, 0xaaaaaaa2),
    (0xbbbb509b, 0xbbbbba7c, 0xbbbb5a9d, 0xbbbbbb7e, 0xbbbbbd9f, 0xbbbbbb7a, 0xbbbbbac0, 0xbbbbbae8,
     0xbbbbbbd5, 0xbbbbbbb7, 0xbbbbbbb1, 0xbbbbbbb4, 0xbbbbbbb3, 0xbbbbbba2, 0xbbbbbbb6, 0xbbbbbbb9),
    (0xcccc5bdc, 0xccccceda, 0xcccccccd, 0xccccccf9, 0xcccccb18, 0xcccccafe, 0xccccdeb7, 0xcccccda1,
     0xcccccae5, 0xccccccc0, 0xcccccccb, 0xccccccc2, 0xccccccc6, 0xccccccc3, 0xcccccccf, 0xccccccc4),
    (0xdddc16bd, 0xddddd10c, 0xddddddce, 0xddddddb0, 0xddddddfa, 0xdddddba4, 0xddddebc2, 0xddddddaf,
     0xddddddb9, 0xddddddf7, 0xddddddd1, 0xddddddf3, 0xdddddddb, 0xddddddd8, 0xddddddd5, 0xddddddd6),
    (0xeeeedb0e, 0xeeeeeebf, 0xeeeeeee0, 0xeeeeeee3, 0xeeeeeeb1, 0xeeeeeeea, 0xeeeeeee4, 0xeeeeedfb,
     0xeeeeeee7, 0xeeeeeeed, 0xeeeeeee2, 0xeeeeeee8, 0xeeeeeee5, 0xeeeeeee6, 0xeeeeeeec, 0xeeeeeee9),
    (0xfff20e3f, 0xfffffff0, 0xffffffe1, 0xfffffed4, 0xfffffff5, 0xfffffff2, 0xfffffff9, 0xfffffffa,
     0xfffffffe, 0xfffffffd, 0xffffffec, 0xfffffffb, 0xfffffff6, 0xfffffff8, 0xfffffff7, 0xfffffff3),
)

def signed(word):
    return word - (1 << 32) if word >= 1 << 31 else word


def by_z(z, values):
    picked = jnp.int32(signed(values[0]))
    for k in range(1, 16):
        if values[k] != values[0]:
            picked = jnp.where(z == k, jnp.int32(signed(values[k])), picked)
    return picked


def nibble(word, k):
    return (word >> (4 * k)) & 15


def quarter(word):
    first = (word & 15) // SPAN * SPAN
    return range(first, first + SPAN)


def targets(z):
    found = []
    for word in TREE[z]:
        for k in range(1, 8):
            d = (word >> (4 * k)) & 15
            if d != z and d not in found:
                found.append(d)
    return found


SENDS = [sum((word >> (4 * k)) & 15 != z for word in TREE[z] for k in range(1, 8)) for z in range(16)]
TARGETS = [len(targets(z)) for z in range(16)]
LAST = [
    sum(1 << k for k in range(16) if all(TREE[z][i] & 15 != q for i in range(k + 1, 16) for q in quarter(TREE[z][k])))
    for z in range(16)
]
GROUPS = tuple(q // SPAN for q in (0, 2, 4, 6, 14, 12, 10, 8)) if SPAN == 2 else (0, 1, 3, 2)
SOURCES = [sum(1 << z for z in range(16) if d in targets(z)) for d in range(16)]


def labels(position, base, occ, vir):
    first = base // NVIR
    orbital = jnp.full_like(position, first)
    for k in (1, 2):
        orbital += (position >= (first + k) * NVIR).astype(jnp.int32)
    virtual = position - orbital * NVIR
    occ_part = jnp.zeros_like(position)
    vir_part = jnp.zeros_like(position)
    occ_bound = jnp.int32(0)
    vir_bound = jnp.int32(0)
    for k in range(7):
        occ_bound += occ[k]
        vir_bound += vir[k]
        occ_part += (orbital >= occ_bound).astype(jnp.int32)
        vir_part += (virtual >= vir_bound).astype(jnp.int32)
    return occ_part ^ vir_part


def split(x):
    high = x.astype(BF16)
    return high, (x - high.astype(F32)).astype(BF16)


def product(left, right):
    dims = (((0,), (0,)), ((), ()))
    lh, ll = split(left)
    rh, rl = split(right)
    dot = lambda a, b: lax.dot_general(a, b, dims, preferred_element_type=F32)
    return dot(lh, rh) + (dot(lh, rl) + dot(ll, rh))


def kernel(
    a_hbm, b_hbm, occ_hbm, vir_hbm, o_ref,
    w, br, bc, ac, row_lab, occ, vir,
    local, w_in, br_in, bc_in, ac_in, cross_in, ap_in, share_in, ready,
    tree_out, cross_out, br_out, bc_out, ac_out, pair_out, ap_out, share_out,
):
    row = lax.axis_index("row")
    col = lax.axis_index("col")
    z = col % 16
    yhi = col // 16
    ylo = row // 8
    core = row % 2
    x = row // 2 % 4

    own = [
        pltpu.make_async_copy(a_hbm.at[:, pl.ds(256 * h, 256)], w.at[col, h], local.at[0])
        for h in (0, 1)
    ] + [
        pltpu.make_async_copy(b_hbm.at[pl.ds(8 * h, 8)], w.at[col, 2 + h], local.at[0])
        for h in (0, 1)
    ]
    small = [
        pltpu.make_async_copy(occ_hbm, occ, local.at[2]),
        pltpu.make_async_copy(vir_hbm, vir, local.at[3]),
        pltpu.make_async_copy(b_hbm.at[pl.ds(0, 8)], bc.at[row, 0], local.at[1]),
        pltpu.make_async_copy(b_hbm.at[pl.ds(8, 8)], bc.at[row, 1], local.at[1]),
    ]
    barrier = pltpu.get_barrier_semaphore()
    sources = by_z(z, SOURCES)

    def greet_z(d, carry):
        @pl.when(((sources >> d) & 1) == 1)
        def _():
            pl.semaphore_signal(
                barrier, inc=1, device_id={"row": row, "col": yhi * 16 + d}, device_id_type=MESH
            )
        return carry

    other = {"row": row + 1 - 2 * core, "col": col}
    peers = [other]
    peers += [{"row": ylo * 8 + (x + k) % 4 * 2 + core, "col": col} for k in (1, 2, 3)]
    peers += [
        {"row": (ylo + k % 2) % 2 * 8 + x * 2 + core, "col": (yhi + k // 2) % 2 * 16 + z} for k in (1, 2, 3)
    ]
    late = z >= 8

    @pl.when(late)
    def _():
        for peer in peers:
            pl.semaphore_signal(barrier, inc=1, device_id=peer, device_id_type=MESH)

    @pl.when(jnp.logical_not(late))
    def _():
        def greet_plane(t, carry):
            r, y = t % 16, t // 16

            @pl.when(jnp.logical_or(r != row, y != yhi))
            def _():
                pl.semaphore_signal(
                    barrier, inc=1, device_id={"row": r, "col": y * 16 + z}, device_id_type=MESH
                )
            return carry

        lax.fori_loop(0, 32, greet_plane, 0)

    lax.fori_loop(0, 16, greet_z, 0)
    for copy in own + small:
        copy.start()

    share = ylo * 8 + (x - z // 4 + 6) % 4 * 2 + core
    early = jnp.logical_not(late)
    shares = jnp.logical_and(early, share % 8 >= 4)
    direct = jnp.logical_and(late, x < 2)

    @pl.when(shares)
    def _():
        for e in (0, 1):
            pl.semaphore_signal(
                barrier, inc=1, device_id={"row": col // 2, "col": 2 * share + e}, device_id_type=MESH
            )

    def label_rows():
        small[0].wait()
        small[1].wait()
        pltpu.make_async_copy(bc.at[0], bc.at[0], local.at[1]).wait()
        row_pos = row * 512 + lax.broadcasted_iota(jnp.int32, (512, 128), 0)
        row_lab[...] = labels(row_pos, row * 512, occ, vir)

    @pl.when(early)
    def _():
        label_rows()

    pl.semaphore_wait(
        barrier, jnp.where(late, 7, 31) + by_z(z, TARGETS) + 2 * direct.astype(jnp.int32)
    )

    @pl.when(late)
    def _():
        for peer in peers:
            pl.semaphore_signal(ready.at[0], inc=1, device_id=peer, device_id_type=MESH)

    pltpu.make_async_copy(w.at[0], w.at[0], local.at[0]).wait()

    def send_tree(s, d):
        c = yhi * 16 + s
        pltpu.make_async_remote_copy(
            src_ref=w.at[c], dst_ref=w.at[c], send_sem=tree_out, recv_sem=w_in.at[s],
            device_id={"row": row, "col": yhi * 16 + d}, device_id_type=MESH,
        ).start()

    def cross(s):
        c = yhi * 16 + s
        return pltpu.make_async_remote_copy(
            src_ref=w.at[c, pl.ds(0, 2)], dst_ref=w.at[c, pl.ds(0, 2)], send_sem=cross_out,
            recv_sem=cross_in, device_id={"row": row, "col": (1 - yhi) * 16 + z}, device_id_type=MESH,
        )

    def to_rows(s, y):
        r = yhi * 8 + s // 2
        source = w.at[yhi * 16 + s, pl.ds(2, 2)]
        me = jnp.logical_and(r == row, y == yhi)

        @pl.when(me)
        def _():
            pltpu.make_async_copy(source, br.at[row, s % 2], br_in).start()

        @pl.when(jnp.logical_not(me))
        def _():
            pltpu.make_async_remote_copy(
                src_ref=source, dst_ref=br.at[row, s % 2], send_sem=br_out, recv_sem=br_in,
                device_id={"row": r, "col": y * 16 + z}, device_id_type=MESH,
            ).start()

    owner = row % 8 == z // 2
    half = z % 2

    def to_plane(g):
        c = yhi * 16 + SPAN * g
        t = yhi * (16 // SPAN) + g
        source = w.at[pl.ds(c, SPAN), half]

        def one(chip, carry):
            r = 2 * chip + core
            me = jnp.logical_and(r == row, ylo == yhi)

            @pl.when(me)
            def _():
                pltpu.make_async_copy(source, ac.at[pl.ds(c, SPAN)], ac_in.at[t]).start()

            @pl.when(jnp.logical_not(me))
            def _():
                pltpu.make_async_remote_copy(
                    src_ref=source, dst_ref=ac.at[pl.ds(c, SPAN)], send_sem=ac_out,
                    recv_sem=ac_in.at[t],
                    device_id={"row": r, "col": ylo * 16 + z}, device_id_type=MESH,
                ).start()
            return carry

        lax.fori_loop(0, 8, one, 0)

    def direct_to(h):
        r = yhi * 8 + (x + z // 4 + 2) % 4 * 2 + z // 2 % 2
        return pltpu.make_async_remote_copy(
            src_ref=w.at[col, h], dst_ref=ac.at[col], send_sem=ap_out, recv_sem=ap_in,
            device_id={"row": r, "col": 2 * row + h}, device_id_type=MESH,
        )

    share_piece = ac.at[pl.ds(2 * share, 2)]

    @pl.when(direct)
    def _():
        direct_to(0).start()
        direct_to(1).start()

    last = by_z(z, LAST)
    for k in range(16):
        word = by_z(z, [TREE[v][k] for v in range(16)])
        s = nibble(word, 0)
        if k:
            pltpu.make_async_copy(w.at[s], w.at[s], w_in.at[s]).wait()

        def forward(i, carry):
            d = (word >> (4 * i)) & 15
            there = d != z

            @pl.when(there)
            def _():
                send_tree(s, d)
            return carry

        lax.fori_loop(1, 8, forward, 0)
        if k == 0:
            @pl.when(late)
            def _():
                pl.semaphore_wait(ready.at[0], 7)
                pl.semaphore_signal(ready.at[1], inc=1, device_id=other, device_id_type=MESH)
                pl.semaphore_wait(ready.at[1], 1)
        @pl.when(
            jnp.logical_and(jnp.logical_and(owner, ((last >> k) & 1) == 1), jnp.logical_or(late, s < 8))
        )
        def _():
            to_plane(s // SPAN)

        cross(s).start()
        to_rows(s, 0)
        to_rows(s, 1)


        if k == 0:
            def give(r, carry):
                @pl.when(r != row)
                def _():
                    pltpu.make_async_remote_copy(
                        src_ref=w.at[col, pl.ds(2, 2)], dst_ref=bc.at[row], send_sem=bc_out,
                        recv_sem=bc_in, device_id={"row": r, "col": col}, device_id_type=MESH,
                    ).start()
                return carry

            lax.fori_loop(0, 16, give, 0)


        if k == SHARE_AFTER:
            @pl.when(shares)
            def _():
                pltpu.make_async_copy(share_piece, share_piece, ap_in).wait()

                def give_share(r, carry):
                    @pl.when(r != row)
                    def _():
                        pltpu.make_async_remote_copy(
                            src_ref=share_piece, dst_ref=share_piece, send_sem=share_out,
                            recv_sem=share_in, device_id={"row": r, "col": col}, device_id_type=MESH,
                        ).start()
                    return carry

                lax.fori_loop(0, 16, give_share, 0)

    first = core == (z // 2) % 2

    def group(t):
        return ac.at[pl.ds(SPAN * t, SPAN)]

    for g in GROUPS:
        @pl.when(jnp.logical_and(first, late) if g * SPAN >= 8 else first)
        def _():
            for y in (0, 1):
                t = 16 // SPAN * y + g
                pltpu.make_async_copy(group(t), group(t), ac_in.at[t]).wait()
                pltpu.make_async_remote_copy(
                    src_ref=group(t), dst_ref=group(t), send_sem=pair_out,
                    recv_sem=ac_in.at[t], device_id={"row": 2 * (row // 2) + 1 - core, "col": col},
                    device_id_type=MESH,
                ).start()

    @pl.when(late)
    def _():
        label_rows()

    pltpu.make_async_copy(bc.at[pl.ds(0, 15)], bc.at[pl.ds(0, 15)], bc_in).wait()
    pltpu.make_async_copy(ac, ac, cross_in).wait()
    b_here = bc[...].reshape(256, 256)
    for m in (0, 1):
        o_ref[256 * m : 256 * (m + 1)] = product(w[:, m].reshape(256, 256), b_here)

    pltpu.make_async_copy(br, br, br_in).wait()

    for t in range(32 // SPAN):
        here = jnp.logical_not(first)

        @pl.when(jnp.logical_and(here, late) if t * SPAN % 16 >= 8 else here)
        def _():
            pltpu.make_async_copy(group(t), group(t), ac_in.at[t]).wait()

    @pl.when(shares)
    def _():
        pltpu.make_async_copy(ac.at[pl.ds(0, 14)], ac.at[pl.ds(0, 14)], share_in).wait()

    @pl.when(jnp.logical_and(early, jnp.logical_not(shares)))
    def _():
        pltpu.make_async_copy(ac.at[pl.ds(0, 16)], ac.at[pl.ds(0, 16)], share_in).wait()

    col_lab = labels(
        col * 256 + lax.broadcasted_iota(jnp.int32, (8, 256), 1), col * 256, occ, vir
    )[:1]
    a_here = ac[...].reshape(256, 256)
    for m in (0, 1):
        rows = slice(256 * m, 256 * (m + 1))
        total = o_ref[rows] + product(br[:, m].reshape(256, 256), a_here)
        lab = row_lab[rows]
        for h in (0, 1):
            lanes = slice(128 * h, 128 * (h + 1))
            o_ref[rows, lanes] = jnp.where(lab == col_lab[:, lanes], total[:, lanes], 0.0)

    count = by_z(z, SENDS)
    for n in sorted(set(SENDS)):
        @pl.when(count == n)
        def _():
            pltpu.make_async_copy(w.at[pl.ds(0, n)], w.at[pl.ds(0, n)], tree_out).wait()

    pltpu.make_async_copy(ac, ac, cross_out).wait()
    pltpu.make_async_copy(bc.at[pl.ds(0, 15)], bc.at[pl.ds(0, 15)], bc_out).wait()

    @pl.when(ylo == yhi)
    def _():
        pltpu.make_async_copy(br.at[pl.ds(0, 15)], br.at[pl.ds(0, 15)], br_out).wait()

    @pl.when(ylo != yhi)
    def _():
        pltpu.make_async_copy(br, br, br_out).wait()

    for when, chips in ((ylo == yhi, 7), (ylo != yhi, 8)):
        for plane, pieces in ((early, 2 * chips), (late, 4 * chips)):
            @pl.when(jnp.logical_and(owner, jnp.logical_and(when, plane)))
            def _():
                pltpu.make_async_copy(w.at[pl.ds(0, pieces)], w.at[pl.ds(0, pieces)], ac_out).wait()

    for plane, pieces in ((early, 16), (late, 32)):
        @pl.when(jnp.logical_and(first, plane))
        def _():
            pltpu.make_async_copy(ac.at[pl.ds(0, pieces)], ac.at[pl.ds(0, pieces)], pair_out).wait()

    @pl.when(direct)
    def _():
        pltpu.make_async_copy(ac.at[pl.ds(0, 2)], ac.at[pl.ds(0, 2)], ap_out).wait()

    @pl.when(shares)
    def _():
        pltpu.make_async_copy(ac.at[pl.ds(0, 30)], ac.at[pl.ds(0, 30)], share_out).wait()


def per_device(amplitudes, integrals, occ_counts, vir_counts):
    arrays = (amplitudes.T, integrals, occ_counts, vir_counts)
    hbm = pl.BlockSpec(memory_space=pltpu.HBM)
    dma = pltpu.SemaphoreType.DMA
    return pl.pallas_call(
        kernel,
        out_shape=jax.ShapeDtypeStruct((512, 256), F32),
        in_specs=[hbm, hbm, hbm, hbm],
        out_specs=pl.BlockSpec(memory_space=pltpu.VMEM),
        scratch_shapes=[
            pltpu.VMEM((32, 4, 8, 256), F32),
            pltpu.VMEM((16, 2, 2, 8, 256), F32),
            pltpu.VMEM((16, 2, 8, 256), F32),
            pltpu.VMEM((32, 8, 256), F32),
            pltpu.VMEM((512, 128), jnp.int32),
            pltpu.SMEM((8,), jnp.int32),
            pltpu.SMEM((8,), jnp.int32),
            dma((4,)), dma((16,)), dma, dma, dma((32 // SPAN,)), dma,
            dma, dma, pltpu.SemaphoreType.REGULAR((2,)),
            dma, dma, dma, dma, dma, dma, dma, dma,
        ],
        compiler_params=pltpu.CompilerParams(
            collective_id=0, has_side_effects=True, vmem_limit_bytes=32 * 2**20
        ),
    )(*[pltpu.with_memory_space_constraint(v, pltpu.HBM) for v in arrays])


def solution(mesh):
    placed = (P("row", "col"), P("row", "col"), P(), P())
    return jax.shard_map(
        per_device, mesh=mesh, in_specs=placed, out_specs=P("row", "col"), check_vma=False
    )
```
